256 devices in a mesh: blk: 8 (over x_hi, y), rep: 32 (over z, x_lo, core).
Axes of the slice: x: 4 (x_hi: 2, x_lo: 2; x = x_hi * 2 + x_lo), y: 4, z: 8, core: 2. Of those that a mesh axis runs over, the one named last changes fastest.
Arguments:
- query_hidden: bfloat16 [32, 32, 32, 768], P('rep', 'blk'), may hold values from -18 to 18
- passage_hidden: bfloat16 [32, 32, 512, 768], P('rep', 'blk'), may hold values from -6 to 6
- lengths: int32 [32, 32], P('rep', 'blk'), may hold values from 64 to 512
- projection: bfloat16 [768, 128], replicated, may hold values from -0.21875 to 0.21875
Outputs:
- query_grad: float32 [32, 32, 32, 128], P('rep', 'blk')
- passage_grad: float32 [32, 32, 512, 128], P('rep', 'blk')
- grad_weight: float32 [768, 128], replicated
- loss: float32 [], replicated
The draws below stay inside these ranges and needn't reach their ends.
All inputs are finite; a program needn't handle non-finite values.
Results may differ from the reference program's by a relative error of at most 0.0097.
Values may be sent and summed in bfloat16 or wider, within the bound.
No kernel may reach another device: no remote copies, remote signals or barrier semaphores. Data moves between devices by JAX's collectives and lax.ppermute only.
A program may use at most 128 MiB of HBM per device.

```python
import jax
import jax.numpy as jnp
from jax import lax

H = 768
DIM = 128
QLEN = 32
PLEN = 512
QN = 32
PN = 32
NQ_ALL = 1024
N_REP = 32


def shared_passages(key):
    noise = jax.random.normal(jax.random.fold_in(key, 11), (N_REP, PN, PLEN, H), jnp.float32)
    values = jnp.clip(noise, -6.0, 6.0)
    return values


def draw_passage_hidden(key, part):
    return shared_passages(key).astype(jnp.bfloat16)


def draw_query_hidden(key, part):
    noise = jax.random.normal(jax.random.fold_in(key, 13), (N_REP, QN, QLEN, H), jnp.float32)
    values = 0.1 * jnp.clip(noise, -6.0, 6.0)
    return values.astype(jnp.bfloat16)


def touch_ends(values, stream_key, least, top_value):
    dims = values.shape
    spot = [jax.random.randint(jax.random.fold_in(stream_key, axis), (), 0, dims[axis]) for axis in range(len(dims))]
    values = values.at[tuple(spot)].set(least)
    longest = dims.index(max(dims))
    spot[longest] = (spot[longest] + 1) % dims[longest]
    return values.at[tuple(spot)].set(top_value)


def bell_draw(key, extent, width, reach, kind=jnp.bfloat16):
    values = jax.random.normal(key, extent, jnp.float32) * width
    return jnp.minimum(jnp.maximum(values, -reach), reach).astype(kind)


def setup_inputs(seed: int = 0) -> dict:
    key_list = jax.random.split(jax.random.key(seed), 5)
    query_hidden = draw_query_hidden(jax.random.fold_in(key_list[4], 71), 0)
    passage_hidden = draw_passage_hidden(jax.random.fold_in(key_list[4], 71), 0)
    lengths = touch_ends(jax.random.randint(key_list[2], (N_REP, PN), PLEN // 8, PLEN + 1), jax.random.fold_in(key_list[2], 1), PLEN // 8, PLEN).astype(jnp.int32)
    projection = bell_draw(key_list[3], (H, DIM), H ** -0.5, 0.21875)
    return dict(query_hidden=query_hidden, passage_hidden=passage_hidden, lengths=lengths, projection=projection)


temper = 0.5


def soft_scores(scores, lens):
    slots = scores.shape[-1]
    valid = lax.broadcasted_iota(jnp.int32, (lens.shape[0], slots), 1) < lens[:, None]
    scaled = jnp.where(valid[None], scores / temper, -jnp.inf)
    top = jnp.max(scaled, -1, keepdims=True)
    logz = top + jnp.log(jnp.sum(jnp.exp(scaled - top), -1, keepdims=True))
    pooled = temper * (logz[..., 0] - jnp.log(lens.astype(jnp.float32))[None])
    return pooled, scaled, logz


def group_step(inputs):
    qhid, phid, lens, projection = inputs
    hidden = projection.shape[0]
    qtok = jnp.dot(qhid.reshape(-1, hidden), projection, preferred_element_type=jnp.float32).astype(jnp.bfloat16)
    ptok = jnp.dot(phid.reshape(-1, hidden), projection, preferred_element_type=jnp.float32).astype(jnp.bfloat16)
    nquery = qhid.shape[0]
    qlen = qhid.shape[1]
    npass = phid.shape[0]
    plen = phid.shape[1]
    scores = jnp.dot(qtok, ptok.T, preferred_element_type=jnp.float32).reshape(nquery * qlen, npass, plen)
    pooled, scaled, logz = soft_scores(scores, lens)
    score = jnp.sum(pooled.reshape(nquery, qlen, npass), 1)
    top = jnp.max(score, 1, keepdims=True)
    lse = top + jnp.log(jnp.sum(jnp.exp(score - top), 1, keepdims=True))
    target = lax.broadcasted_iota(jnp.int32, score.shape, 1) == lax.broadcasted_iota(jnp.int32, score.shape, 0)
    loss_part = jnp.sum(lse[:, 0] - jnp.sum(jnp.where(target, score, 0.0), 1))
    dscore = (jnp.exp(score - lse) - target.astype(jnp.float32)) / NQ_ALL
    spread = jnp.repeat(dscore, qlen, axis=0)
    grad_a = (spread[:, :, None] * jnp.exp(scaled - logz)).astype(jnp.bfloat16).reshape(nquery * qlen, npass * plen)
    qgrad = jnp.dot(grad_a, ptok, preferred_element_type=jnp.float32)
    pgrad = jnp.dot(grad_a.T, qtok, preferred_element_type=jnp.float32)
    wgrad = jnp.dot(qhid.reshape(-1, hidden).T, qgrad.astype(jnp.bfloat16), preferred_element_type=jnp.float32)
    wgrad = wgrad + jnp.dot(phid.reshape(-1, hidden).T, pgrad.astype(jnp.bfloat16), preferred_element_type=jnp.float32)
    return qgrad.reshape(nquery, qlen, -1), pgrad.reshape(npass, plen, -1), wgrad, loss_part


def reference(query_hidden, passage_hidden, lengths, projection):
    copies = jnp.broadcast_to(projection, (query_hidden.shape[0],) + projection.shape)
    qgrad, pgrad, wgrad, losses = lax.map(group_step, (query_hidden, passage_hidden, lengths, copies))
    return qgrad, pgrad, jnp.sum(wgrad, 0), jnp.sum(losses) / NQ_ALL
```

```python
import functools
import math

import jax
import jax.numpy as jnp
from jax import lax
from jax.experimental import pallas as pl
from jax.experimental.pallas import tpu as pltpu
from jax.sharding import PartitionSpec as P

F32 = jnp.float32
BF16 = jnp.bfloat16
INV_TEMPER = 2.0
TEMPER = 0.5
LANES = 128
EXTRA = 32
NN = (((1,), (0,)), ((), ()))
NT = (((1,), (1,)), ((), ()))
TN = (((0,), (0,)), ((), ()))


def mm(a, b, dims):
    return lax.dot_general(a, b, dims, preferred_element_type=F32)


def to_row(x):
    return jnp.concatenate([x[c : c + 1, :] for c in range(x.shape[0])], axis=1)


def to_chunks(x):
    n = x.shape[1] // LANES
    return jnp.concatenate([x[:, c * LANES : (c + 1) * LANES] for c in range(n)], axis=0)


def split3(x):
    hi = x.astype(BF16).astype(F32)
    rest = x - hi
    mid = rest.astype(BF16).astype(F32)
    return hi, mid, (rest - mid)


def segment_sum(x, width):
    lane = lax.broadcasted_iota(jnp.int32, x.shape, 1)
    step = 1
    while step < width:
        up = pltpu.roll(x, x.shape[1] - step, 1)
        down = pltpu.roll(x, step, 1)
        x = x + jnp.where((lane & step) == 0, up, down)
        step *= 2
    return x


def query_kernel(q_ref, w_ref, out_ref):
    tok = mm(q_ref[...], w_ref[...], NN)
    flipped = tok.T.astype(BF16)
    for c in range(out_ref.shape[0]):
        out_ref[c] = flipped


def score_kernel(qlen, len_ref, me_ref, qt_ref, phid_ref, w_ref, e_ref, stat_ref, send_ref, own_ref, qs_ref, g_ref):
    p = pl.program_id(0)
    nblk = qt_ref.shape[0]
    slots = phid_ref.shape[1]
    npass = stat_ref.shape[1]

    @pl.when(p == 0)
    def _():
        for c in range(nblk):
            qs_ref[:, c * LANES : (c + 1) * LANES] = qt_ref[c]

    ptok = mm(phid_ref[0], w_ref[...], NN)
    pvec = ptok.astype(BF16)
    pvec_t = ptok.T.astype(BF16)
    count = len_ref[p]
    scores = mm(pvec, qs_ref[...], NN)
    row = lax.broadcasted_iota(jnp.int32, scores.shape, 0)
    scores = jnp.where(row < count, scores, -jnp.inf)
    top = jnp.max(scores, axis=0, keepdims=True)
    e = jnp.exp2((scores - top) * (INV_TEMPER * math.log2(math.e)))
    total = jnp.sum(e, axis=0, keepdims=True)
    eb = e.astype(BF16)
    e_ref[0] = eb
    inv = 1.0 / total
    g = mm(pvec_t, eb, NN) * inv
    for c in range(nblk):
        g_ref[p, c] = g[:, c * LANES : (c + 1) * LANES]
    logz = to_chunks(top * INV_TEMPER + jnp.log(total))
    log_count = jnp.log(jnp.full(logz.shape, count, jnp.int32).astype(F32))
    stat_ref[0, p] = segment_sum(TEMPER * (logz - log_count), qlen)
    stat_ref[1, p] = to_chunks(inv)

    @pl.when(p == npass - 1)
    def _():
        score = [stat_ref[0, k] for k in range(npass)]
        high = functools.reduce(jnp.maximum, score)
        lse = high + jnp.log(sum(jnp.exp(s - high) for s in score))
        share = [jnp.exp(s - lse) for s in score]
        hi, mid, lo = split3(lse)
        extra = jnp.concatenate([hi, mid, lo, jnp.zeros_like(lo)], axis=0).astype(BF16)
        for c in range(nblk):
            part = sum(g_ref[k, c] * share[k][c : c + 1, :] for k in range(npass))
            send_ref[c, :LANES, :] = part.astype(BF16)
            send_ref[c, LANES:, :] = extra
        me = me_ref[0]
        for k in range(npass):
            own_ref[k] = g_ref[k, me]


def grad_kernel(
    qlen, total, len_ref, me_ref, recv_ref, e_ref, stat_ref, own_ref, qt_ref, phid_ref, qhid_ref,
    qgrad_ref, pgrad_ref, send_ref, lse_ref, acc_ref, qs_ref,
):
    p = pl.program_id(0)
    nblk = qt_ref.shape[0]
    npass = stat_ref.shape[1]
    me = me_ref[0]
    lane = lax.broadcasted_iota(jnp.int32, (nblk, LANES), 1)
    chunk = lax.broadcasted_iota(jnp.int32, (nblk, LANES), 0)
    mine = chunk == me

    def pick(x):
        return jnp.sum(jnp.where(mine, x, 0.0), axis=0, keepdims=True)

    def dscore_of(k, lse):
        hit = mine & (lane // qlen == k)
        return (jnp.exp(stat_ref[0, k] - lse) - hit.astype(F32)) / total

    @pl.when(p == 0)
    def _():
        parts = []
        for d in range(nblk):
            x = recv_ref[d, LANES:, :].astype(F32)
            parts.append(x[:nblk] + x[nblk : 2 * nblk] + x[2 * nblk : 3 * nblk])
        high = functools.reduce(jnp.maximum, parts)
        lse = high + jnp.log(sum(jnp.exp(x - high) for x in parts))
        lse_ref[...] = lse
        grad = jnp.zeros((LANES, LANES), F32)
        for k in range(npass):
            grad = grad + own_ref[k] * pick(dscore_of(k, lse))
        for d in range(nblk):
            share = jnp.where(me == d, 0.0, pick(jnp.exp(parts[d] - lse)) / total)
            grad = grad + recv_ref[d, :LANES, :].astype(F32) * share
        grad = grad.T
        qgrad_ref[...] = grad
        acc_ref[...] = mm(qhid_ref[...], grad.astype(BF16), TN)

    lse = lse_ref[...]
    weight = dscore_of(p, lse) * stat_ref[1, p]
    for c in range(nblk):
        qs_ref[:, c * LANES : (c + 1) * LANES] = (qt_ref[c].astype(F32) * weight[c : c + 1, :]).astype(BF16)
    pgrad = mm(e_ref[0], qs_ref[...], NT)
    pgrad_ref[0] = pgrad
    acc_ref[...] += mm(phid_ref[0], pgrad.astype(BF16), TN)

    @pl.when(p == npass - 1)
    def _():
        loss = jnp.zeros((nblk, LANES), F32)
        for k in range(npass):
            first = mine & (lane == k * qlen)
            loss = loss + jnp.where(first, lse - stat_ref[0, k], 0.0)
        hi, mid, lo = split3(jnp.full((1, LANES), jnp.sum(loss)))
        extra = jnp.concatenate([hi, mid, lo, jnp.zeros((5, LANES), F32)], axis=0)
        nrep, rows = send_ref.shape[0], send_ref.shape[1] - 8
        for r in range(nrep):
            send_ref[r] = jnp.concatenate([acc_ref[r * rows : (r + 1) * rows, :], extra], axis=0).astype(BF16)


def sum_spread_kernel(x_ref, out_ref):
    y = jnp.sum(x_ref[...].astype(F32), axis=0)
    for c in range(out_ref.shape[0]):
        out_ref[c] = y


def sum_final_kernel(total, x_ref, out_ref, loss_ref):
    y = jnp.sum(x_ref[...], axis=0)
    rows = out_ref.shape[1]
    z = y[:rows].astype(BF16)
    for c in range(out_ref.shape[0]):
        out_ref[c] = z
    loss_ref[...] = jnp.sum(y[rows:], axis=0, keepdims=True) / total


def params(mib=48):
    return pltpu.CompilerParams(vmem_limit_bytes=mib << 20)


VM = pl.BlockSpec(memory_space=pltpu.VMEM)
SM = pl.BlockSpec(memory_space=pltpu.SMEM)


def whole(shape):
    return pl.BlockSpec(shape, lambda p: (0,) * len(shape))


def shards(query_hidden, passage_hidden, lengths, projection):
    hidden, dim = projection.shape
    nquery, qlen = query_hidden.shape[1:3]
    npass, plen = passage_hidden.shape[1:3]
    nblk, nrep = lax.axis_size("blk"), lax.axis_size("rep")
    total = nblk * nrep * nquery
    ntok = nblk * nquery * qlen
    qflat = query_hidden[0].reshape(-1, hidden)
    phid = passage_hidden[0]
    lens = lengths[0]
    me = lax.axis_index("blk").astype(jnp.int32)[None]

    copies = pl.pallas_call(
        query_kernel,
        name="query_tokens",
        out_shape=jax.ShapeDtypeStruct((nblk, dim, nquery * qlen), BF16),
        in_specs=[VM, VM],
        out_specs=VM,
        compiler_params=params(),
    )(qflat, projection)
    qt = lax.all_to_all(copies, "blk", 0, 0)

    e, stat, send, own = pl.pallas_call(
        functools.partial(score_kernel, qlen),
        name="scores",
        grid=(npass,),
        out_shape=(
            jax.ShapeDtypeStruct((npass, plen, ntok), BF16),
            jax.ShapeDtypeStruct((2, npass, nblk, LANES), F32),
            jax.ShapeDtypeStruct((nblk, dim + EXTRA, LANES), BF16),
            jax.ShapeDtypeStruct((npass, dim, LANES), F32),
        ),
        in_specs=[
            SM,
            SM,
            whole((nblk, dim, LANES)),
            pl.BlockSpec((1, plen, hidden), lambda p: (p, 0, 0)),
            whole((hidden, dim)),
        ],
        out_specs=(
            pl.BlockSpec((1, plen, ntok), lambda p: (p, 0, 0)),
            whole((2, npass, nblk, LANES)),
            whole((nblk, dim + EXTRA, LANES)),
            whole((npass, dim, LANES)),
        ),
        scratch_shapes=[pltpu.VMEM((dim, ntok), BF16), pltpu.VMEM((npass, nblk, dim, LANES), F32)],
        compiler_params=params(),
    )(lens, me, qt, phid, projection)
    recv = lax.all_to_all(send, "blk", 0, 0)

    rows = hidden // nrep
    qgrad, pgrad, send = pl.pallas_call(
        functools.partial(grad_kernel, qlen, float(total)),
        name="grads",
        grid=(npass,),
        out_shape=(
            jax.ShapeDtypeStruct((nquery * qlen, dim), F32),
            jax.ShapeDtypeStruct((npass, plen, dim), F32),
            jax.ShapeDtypeStruct((nrep, rows + 8, dim), BF16),
        ),
        in_specs=[
            SM,
            SM,
            whole((nblk, dim + EXTRA, LANES)),
            pl.BlockSpec((1, plen, ntok), lambda p: (p, 0, 0)),
            whole((2, npass, nblk, LANES)),
            whole((npass, dim, LANES)),
            whole((nblk, dim, LANES)),
            pl.BlockSpec((1, plen, hidden), lambda p: (p, 0, 0)),
            whole((nquery * qlen, hidden)),
        ],
        out_specs=(
            whole((nquery * qlen, dim)),
            pl.BlockSpec((1, plen, dim), lambda p: (p, 0, 0)),
            whole((nrep, rows + 8, dim)),
        ),
        scratch_shapes=[
            pltpu.VMEM((nblk, LANES), F32),
            pltpu.VMEM((hidden, dim), F32),
            pltpu.VMEM((dim, ntok), BF16),
        ],
        compiler_params=params(),
    )(lens, me, recv, e, stat, own, qt, phid, qflat)

    part = lax.all_to_all(send, "rep", 0, 0)
    part = pl.pallas_call(
        sum_spread_kernel,
        name="sum_rep",
        out_shape=jax.ShapeDtypeStruct((nblk, rows + 8, dim), F32),
        in_specs=[VM],
        out_specs=VM,
        compiler_params=params(),
    )(part)
    part = lax.all_to_all(part, "blk", 0, 0)
    part, loss = pl.pallas_call(
        functools.partial(sum_final_kernel, float(total)),
        name="sum_blk",
        out_shape=(jax.ShapeDtypeStruct((nrep, rows, dim), BF16), jax.ShapeDtypeStruct((1, dim), F32)),
        in_specs=[VM],
        out_specs=(VM, VM),
        compiler_params=params(),
    )(part)
    wgrad = lax.all_to_all(part, "rep", 0, 0).astype(F32).reshape(hidden, dim)
    return (
        qgrad.reshape(1, nquery, qlen, dim),
        pgrad.reshape(1, npass, plen, dim),
        wgrad,
        loss[0, 0],
    )


def solution(mesh):
    return jax.shard_map(
        shards,
        mesh=mesh,
        in_specs=(P("rep", "blk", None, None), P("rep", "blk", None, None), P("rep", "blk"), P()),
        out_specs=(P("rep", "blk", None, None), P("rep", "blk", None, None), P(), P()),
        check_vma=False,
    )
```

```python
import functools
import math

import jax
import jax.numpy as jnp
from jax import lax
from jax.experimental import pallas as pl
from jax.experimental.pallas import tpu as pltpu
from jax.sharding import Mesh
from jax.sharding import PartitionSpec as P

F32 = jnp.float32
BF16 = jnp.bfloat16
INV_TEMPER = 2.0
TEMPER = 0.5
EXP2_SCALE = INV_TEMPER * math.log2(math.e)
LANES = 128
EXTRA = 32
AXES = ("x_hi", "y", "z", "x_lo", "core")
BLK = ("x_hi", "y")
REP = ("z", "x_lo", "core")
PLANE = ("x_hi", "y", "x_lo")
COLUMN = ("z", "core")
NN = (((1,), (0,)), ((), ()))
NT = (((1,), (1,)), ((), ()))
TN = (((0,), (0,)), ((), ()))


def mm(a, b, dims):
    return lax.dot_general(a, b, dims, preferred_element_type=F32)


def to_row(x):
    return jnp.concatenate([x[c : c + 1, :] for c in range(x.shape[0])], axis=1)


def to_chunks(x):
    n = x.shape[1] // LANES
    return jnp.concatenate([x[:, c * LANES : (c + 1) * LANES] for c in range(n)], axis=0)


def split3(x):
    hi = x.astype(BF16).astype(F32)
    rest = x - hi
    mid = rest.astype(BF16).astype(F32)
    return hi, mid, (rest - mid)


def segment_sum(x, width):
    lane = lax.broadcasted_iota(jnp.int32, x.shape, 1)
    step = 1
    while step < width:
        up = pltpu.roll(x, x.shape[1] - step, 1)
        down = pltpu.roll(x, step, 1)
        x = x + jnp.where((lane & step) == 0, up, down)
        step *= 2
    return x


def query_kernel(q_hbm, w_hbm, out_ref, q_ref, w_ref, sem):
    copies = [pltpu.make_async_copy(q_hbm, q_ref, sem.at[0]), pltpu.make_async_copy(w_hbm, w_ref, sem.at[1])]
    for copy in copies:
        copy.start()
    for copy in copies:
        copy.wait()
    tok = mm(q_ref[...], w_ref[...], NN)
    flipped = tok.T.astype(BF16)
    for c in range(out_ref.shape[0]):
        out_ref[c] = flipped


def passage_kernel(len_ref, me_ref, phid_hbm, w_hbm, tok_ref, tab_ref, phid_ref, w_ref, sem):
    npass = phid_ref.shape[0]
    copies = [pltpu.make_async_copy(w_hbm, w_ref, sem.at[npass])]
    copies += [pltpu.make_async_copy(phid_hbm.at[p], phid_ref.at[p], sem.at[p]) for p in range(npass)]
    for copy in copies:
        copy.start()
    shape = tab_ref.shape[1:]
    for p in range(npass):
        tab_ref[p] = jnp.full(shape, len_ref[p], jnp.int32)
    tab_ref[npass] = jnp.full(shape, me_ref[0], jnp.int32)
    copies[0].wait()
    for p in range(npass):
        copies[p + 1].wait()
        tok = mm(phid_ref[p], w_ref[...], NN)
        tok_ref[p, 0] = tok.astype(BF16)
        for r in range(0, tok.shape[0], LANES):
            tok_ref[p, 1, r : r + LANES, :] = tok[r : r + LANES, :].T.astype(BF16)


def score_kernel(qlen, qt_ref, tok_ref, tab_ref, e_ref, stat_ref, send_ref, own_ref, qs_ref, s_ref, g_ref):
    nblk = qt_ref.shape[0]
    npass, slots, ntok = e_ref.shape
    for c in range(nblk):
        qs_ref[:, c * LANES : (c + 1) * LANES] = qt_ref[c]
    rows = 128

    def fold(x, op):
        return functools.reduce(op, [x[r : r + 8] for r in range(0, x.shape[0], 8)])

    def scores(p):
        top = None
        count = tab_ref[p, :1, :1]
        for r in range(0, slots, rows):
            x = mm(tok_ref[p, 0, r : r + rows, :], qs_ref[...], NN)
            row = lax.broadcasted_iota(jnp.int32, (rows, 1), 0) + r
            x = jnp.where(row < count, x, -jnp.inf)
            s_ref[p % 2, r : r + rows, :] = x
            high = fold(x, jnp.maximum)
            top = high if top is None else jnp.maximum(top, high)
        return jnp.max(top, axis=0, keepdims=True)

    def powers(p, top):
        total = jnp.zeros((8, ntok), F32)
        for r in range(0, slots, 16):
            e = jnp.exp2((s_ref[p % 2, r : r + 16, :] - top) * EXP2_SCALE)
            total = total + fold(e, jnp.add)
            e_ref[p, r : r + 16, :] = e.astype(BF16)
        return jnp.sum(total, axis=0, keepdims=True)

    def finish(p, top, total):
        inv = 1.0 / total
        flipped = jnp.concatenate([tok_ref[p, 1, r : r + LANES, :] for r in range(0, slots, LANES)], axis=1)
        g = mm(flipped, e_ref[p], NN) * inv
        for c in range(nblk):
            g_ref[p, c] = g[:, c * LANES : (c + 1) * LANES]
        logz = to_chunks(top * INV_TEMPER + jnp.log(total))
        log_count = jnp.log(tab_ref[p].astype(F32))
        stat_ref[0, p] = segment_sum(TEMPER * (logz - log_count), qlen)
        stat_ref[1, p] = to_chunks(inv)

    top = scores(0)
    for p in range(npass):
        after = scores(p + 1) if p + 1 < npass else None
        total = powers(p, top)
        finish(p, top, total)
        top = after

    score = [stat_ref[0, k] for k in range(npass)]
    high = functools.reduce(jnp.maximum, score)
    lse = high + jnp.log(sum(jnp.exp(s - high) for s in score))
    share = [jnp.exp(s - lse) for s in score]
    hi, mid, lo = split3(lse)
    extra = jnp.concatenate([hi, mid, lo, jnp.zeros_like(lo)], axis=0).astype(BF16)
    me = tab_ref[npass, :1, :1]
    own = [jnp.zeros(own_ref.shape[1:], F32) for _ in range(npass)]
    for c in range(nblk):
        part = jnp.zeros(own_ref.shape[1:], F32)
        for k in range(npass):
            g = g_ref[k, c]
            part = part + g * share[k][c : c + 1, :]
            own[k] = jnp.where(me == c, g, own[k])
        send_ref[c, :LANES, :] = part.astype(BF16)
        send_ref[c, LANES:, :] = extra
    for k in range(npass):
        own_ref[k] = own[k]


def grad_kernel(
    qlen, total, tab_ref, recv_ref, e_ref, stat_ref, own_ref, qt_ref, phid_hbm, qhid_hbm,
    qgrad_ref, pgrad_ref, send_ref, acc_ref, qs_ref, phid_ref, qhid_ref, sem,
):
    nblk = qt_ref.shape[0]
    npass = stat_ref.shape[1]
    copies = [pltpu.make_async_copy(phid_hbm.at[p], phid_ref.at[p], sem.at[p]) for p in range(npass)]
    copies.append(pltpu.make_async_copy(qhid_hbm, qhid_ref, sem.at[npass]))
    for copy in copies:
        copy.start()
    me = tab_ref[npass, :1, :1]
    lane = lax.broadcasted_iota(jnp.int32, (nblk, LANES), 1)
    chunk = lax.broadcasted_iota(jnp.int32, (nblk, LANES), 0)
    mine = chunk == me

    def pick(x):
        return jnp.sum(jnp.where(mine, x, 0.0), axis=0, keepdims=True)

    parts = []
    for d in range(nblk):
        x = recv_ref[d, LANES:, :].astype(F32)
        parts.append(x[:nblk] + x[nblk : 2 * nblk] + x[2 * nblk : 3 * nblk])
    high = functools.reduce(jnp.maximum, parts)
    lse = high + jnp.log(sum(jnp.exp(x - high) for x in parts))
    dscore = []
    loss = jnp.zeros((nblk, LANES), F32)
    for k in range(npass):
        hit = mine & (lane // qlen == k)
        dscore.append((jnp.exp(stat_ref[0, k] - lse) - hit.astype(F32)) / total)
        loss = loss + jnp.where(mine & (lane == k * qlen), lse - stat_ref[0, k], 0.0)

    for p in range(npass):
        weight = dscore[p] * stat_ref[1, p]
        for c in range(nblk):
            qs_ref[p % 2, :, c * LANES : (c + 1) * LANES] = (
                qt_ref[c].astype(F32) * weight[c : c + 1, :]
            ).astype(BF16)
        pgrad = mm(e_ref[p], qs_ref[p % 2], NT)
        pgrad_ref[p] = pgrad
        copies[p].wait()
        term = mm(pgrad.astype(BF16), phid_ref[p], TN)
        if p == 0:
            acc_ref[...] = term
        else:
            acc_ref[...] += term

    grad = jnp.zeros((LANES, LANES), F32)
    for k in range(npass):
        grad = grad + own_ref[k] * pick(dscore[k])
    for d in range(nblk):
        share = jnp.where(me == d, 0.0, pick(jnp.exp(parts[d] - lse)) / total)
        grad = grad + recv_ref[d, :LANES, :].astype(F32) * share
    qgrad_ref[...] = grad.T
    copies[npass].wait()
    wgrad = (acc_ref[...] + mm(grad.astype(BF16), qhid_ref[...], NN)).T

    hi, mid, lo = split3(jnp.full((1, LANES), jnp.sum(loss)))
    extra = jnp.concatenate([hi, mid, lo, jnp.zeros((5, LANES), F32)], axis=0)
    rows = send_ref.shape[1] - 8
    for r in range(send_ref.shape[0]):
        send_ref[r] = jnp.concatenate([wgrad[r * rows : (r + 1) * rows, :], extra], axis=0).astype(BF16)


def sum_spread_kernel(x_ref, out_ref):
    y = jnp.sum(x_ref[...].astype(F32), axis=0)
    rows = y.shape[0] - 8
    hi, mid, lo = split3(jnp.sum(y[rows:], axis=0, keepdims=True))
    y = jnp.concatenate([y[:rows], hi, mid, lo, jnp.zeros((5, LANES), F32)], axis=0).astype(BF16)
    for c in range(out_ref.shape[0]):
        out_ref[c] = y


def sum_final_kernel(total, x_ref, out_ref, loss_ref):
    y = jnp.sum(x_ref[...].astype(F32), axis=0)
    rows = out_ref.shape[1]
    z = y[:rows].astype(BF16)
    for c in range(out_ref.shape[0]):
        out_ref[c] = z
    loss_ref[...] = jnp.sum(y[rows:], axis=0, keepdims=True) / total


def widen_kernel(x_ref, out_ref):
    rows = x_ref.shape[1]
    for c in range(x_ref.shape[0]):
        out_ref[c * rows : (c + 1) * rows, :] = x_ref[c].astype(F32)


VM = pl.BlockSpec(memory_space=pltpu.VMEM)
SM = pl.BlockSpec(memory_space=pltpu.SMEM)
HBM = pl.BlockSpec(memory_space=pltpu.HBM)


def call(name, kernel, ins, out_shape, *args, scratch=(), flops=0, bytes_accessed=0):
    args = [pltpu.with_memory_space_constraint(a, pltpu.HBM) if i is HBM else a for a, i in zip(args, ins)]
    return pl.pallas_call(
        kernel,
        name=name,
        out_shape=out_shape,
        in_specs=ins,
        out_specs=jax.tree.map(lambda _: VM, out_shape),
        scratch_shapes=scratch,
        compiler_params=pltpu.CompilerParams(vmem_limit_bytes=32 << 20),
        cost_estimate=pl.CostEstimate(flops=flops, bytes_accessed=bytes_accessed, transcendentals=0),
    )(*args)


def shards(query_hidden, passage_hidden, lengths, projection):
    hidden, dim = projection.shape
    nquery, qlen = query_hidden.shape[1:3]
    npass, plen = passage_hidden.shape[1:3]
    nblk, nrep = lax.axis_size(BLK), lax.axis_size(REP)
    nplane, ncolumn = lax.axis_size(PLANE), lax.axis_size(COLUMN)
    total = nblk * nrep * nquery
    mine = nquery * qlen
    ntok = nblk * mine
    rows = hidden // nplane
    qflat = query_hidden[0].reshape(-1, hidden)
    me = lax.axis_index(BLK).astype(jnp.int32)[None]
    S = jax.ShapeDtypeStruct

    copies = call(
        "query_tokens", query_kernel, [HBM, HBM], S((nblk, dim, mine), BF16), qflat, projection,
        scratch=[pltpu.VMEM((mine, hidden), BF16), pltpu.VMEM((hidden, dim), BF16), pltpu.SemaphoreType.DMA((2,))],
        flops=2 * mine * hidden * dim, bytes_accessed=400_000,
    )
    qt = lax.all_to_all(copies, BLK, 0, 0)
    tok, tab = call(
        "passage_tokens", passage_kernel, [SM, SM, HBM, HBM],
        (S((npass, 2, plen, dim), BF16), S((npass + 1, nblk, LANES), jnp.int32)),
        lengths[0], me, passage_hidden[0], projection,
        scratch=[pltpu.VMEM((npass, plen, hidden), BF16), pltpu.VMEM((hidden, dim), BF16),
                 pltpu.SemaphoreType.DMA((npass + 1,))],
        flops=2 * npass * plen * hidden * dim, bytes_accessed=8_000_000,
    )
    e, stat, send, own = call(
        "scores", functools.partial(score_kernel, qlen), [VM] * 3,
        (S((npass, plen, ntok), BF16), S((2, npass, nblk, LANES), F32), S((nblk, dim + EXTRA, LANES), BF16),
         S((npass, dim, LANES), F32)),
        qt, tok, tab,
        scratch=[pltpu.VMEM((dim, ntok), BF16), pltpu.VMEM((2, plen, ntok), F32),
                 pltpu.VMEM((npass, nblk, dim, LANES), F32)],
        flops=4 * npass * plen * ntok * dim, bytes_accessed=8_000_000,
    )
    recv = lax.all_to_all(send, BLK, 0, 0)
    qgrad, pgrad, send = call(
        "grads", functools.partial(grad_kernel, qlen, float(total)), [VM] * 6 + [HBM] * 2,
        (S((mine, dim), F32), S((npass, plen, dim), F32), S((nplane, rows + 8, dim), BF16)),
        tab, recv, e, stat, own, qt, passage_hidden[0], qflat,
        scratch=[pltpu.VMEM((dim, hidden), F32), pltpu.VMEM((2, dim, ntok), BF16), pltpu.VMEM((npass, plen, hidden), BF16),
                 pltpu.VMEM((mine, hidden), BF16), pltpu.SemaphoreType.DMA((npass + 1,))],
        flops=2 * npass * plen * ntok * dim, bytes_accessed=8_000_000,
    )
    part = lax.all_to_all(send, PLANE, 0, 0)
    part = call("sum_plane", sum_spread_kernel, [VM], S((ncolumn, rows + 8, dim), BF16), part)
    part = lax.all_to_all(part, COLUMN, 0, 0)
    part, loss = call(
        "sum_column", functools.partial(sum_final_kernel, float(total)), [VM],
        (S((nplane, rows, dim), BF16), S((1, dim), F32)), part,
    )
    wgrad = call("widen", widen_kernel, [VM], S((hidden, dim), F32), lax.all_to_all(part, PLANE, 0, 0))
    return (
        qgrad.reshape(1, nquery, qlen, dim),
        pgrad.reshape(1, npass, plen, dim),
        wgrad,
        loss[0, 0],
    )


def solution(mesh):
    fine = Mesh(mesh.devices.reshape(2, 4, 8, 2, 2), AXES)
    return jax.shard_map(
        shards,
        mesh=fine,
        in_specs=(P(REP, BLK, None, None), P(REP, BLK, None, None), P(REP, BLK), P()),
        out_specs=(P(REP, BLK, None, None), P(REP, BLK, None, None), P(), P()),
        check_vma=False,
    )
```

```python
import functools
import math

import jax
import jax.numpy as jnp
from jax import lax
from jax.experimental import pallas as pl
from jax.experimental.pallas import tpu as pltpu
from jax.sharding import Mesh
from jax.sharding import PartitionSpec as P

F32 = jnp.float32
BF16 = jnp.bfloat16
INV_TEMPER = 2.0
TEMPER = 0.5
EXP2_SCALE = INV_TEMPER * math.log2(math.e)
LANES = 128
EXTRA = 8
AXES = ("x_hi", "y", "z", "x_lo", "core")
BLK = ("x_hi", "y")
REP = ("z", "x_lo", "core")
PLANE = ("x_hi", "y", "x_lo", "core")
COLUMN = "z"
NN = (((1,), (0,)), ((), ()))
NT = (((1,), (1,)), ((), ()))
TN = (((0,), (0,)), ((), ()))


def mm(a, b, dims):
    return lax.dot_general(a, b, dims, preferred_element_type=F32)


def to_row(x):
    return jnp.concatenate([x[c : c + 1, :] for c in range(x.shape[0])], axis=1)


def to_chunks(x):
    n = x.shape[1] // LANES
    return jnp.concatenate([x[:, c * LANES : (c + 1) * LANES] for c in range(n)], axis=0)


def split3(x):
    hi = x.astype(BF16).astype(F32)
    rest = x - hi
    mid = rest.astype(BF16).astype(F32)
    return hi, mid, (rest - mid)


def segment_sum(x, width):
    lane = lax.broadcasted_iota(jnp.int32, x.shape, 1)
    step = 1
    while step < width:
        up = pltpu.roll(x, x.shape[1] - step, 1)
        down = pltpu.roll(x, step, 1)
        x = x + jnp.where((lane & step) == 0, up, down)
        step *= 2
    return x


def query_kernel(q_hbm, w_hbm, out_ref, q_ref, w_ref, sem):
    copies = [pltpu.make_async_copy(q_hbm, q_ref, sem.at[0]), pltpu.make_async_copy(w_hbm, w_ref, sem.at[1])]
    for copy in copies:
        copy.start()
    for copy in copies:
        copy.wait()
    tok = mm(q_ref[...], w_ref[...], NN)
    flipped = tok.T.astype(BF16)
    for c in range(out_ref.shape[0]):
        out_ref[c] = flipped


def passage_kernel(len_hbm, phid_hbm, w_hbm, tok_ref, tab_ref, phid_ref, w_ref, len_ref, sem):
    npass = phid_ref.shape[0]
    lens = pltpu.make_async_copy(len_hbm, len_ref, sem.at[npass + 1])
    lens.start()
    copies = [pltpu.make_async_copy(w_hbm, w_ref, sem.at[npass])]
    copies += [pltpu.make_async_copy(phid_hbm.at[p], phid_ref.at[p], sem.at[p]) for p in range(npass)]
    for copy in copies:
        copy.start()
    shape = tab_ref.shape[1:]
    tab_ref[npass] = jnp.full(shape, lax.axis_index("x_hi") * lax.axis_size("y") + lax.axis_index("y"), jnp.int32)
    lens.wait()
    for p in range(npass):
        tab_ref[p] = jnp.full(shape, len_ref[0, p], jnp.int32)
    copies[0].wait()
    for p in range(npass):
        copies[p + 1].wait()
        tok = mm(phid_ref[p], w_ref[...], NN)
        tok_ref[p, 0] = tok.astype(BF16)
        for r in range(0, tok.shape[0], LANES):
            tok_ref[p, 1, r : r + LANES, :] = tok[r : r + LANES, :].T.astype(BF16)


def score_kernel(qlen, qt_ref, tok_ref, tab_ref, e_ref, stat_ref, send_ref, own_ref, qs_ref, s_ref, g_ref):
    nblk = qt_ref.shape[0]
    npass, slots, ntok = e_ref.shape
    for c in range(nblk):
        qs_ref[:, c * LANES : (c + 1) * LANES] = qt_ref[c]
    rows = 128

    def fold(x, op):
        return functools.reduce(op, [x[r : r + 8] for r in range(0, x.shape[0], 8)])

    def scores(p):
        top = None
        count = tab_ref[p, :1, :1]
        for r in range(0, slots, rows):
            x = mm(tok_ref[p, 0, r : r + rows, :], qs_ref[...], NN)
            row = lax.broadcasted_iota(jnp.int32, (rows, 1), 0) + r
            x = jnp.where(row < count, x, -jnp.inf)
            s_ref[p % 2, r : r + rows, :] = x
            high = fold(x, jnp.maximum)
            top = high if top is None else jnp.maximum(top, high)
        return jnp.max(top, axis=0, keepdims=True)

    def powers(p, top):
        total = jnp.zeros((8, ntok), F32)
        for r in range(0, slots, 16):
            e = jnp.exp2((s_ref[p % 2, r : r + 16, :] - top) * EXP2_SCALE)
            total = total + fold(e, jnp.add)
            e_ref[p, r : r + 16, :] = e.astype(BF16)
        return jnp.sum(total, axis=0, keepdims=True)

    def finish(p, top, total):
        inv = 1.0 / total
        flipped = jnp.concatenate([tok_ref[p, 1, r : r + LANES, :] for r in range(0, slots, LANES)], axis=1)
        g = mm(flipped, e_ref[p], NN) * inv
        for c in range(nblk):
            g_ref[p, c] = g[:, c * LANES : (c + 1) * LANES]
        logz = to_chunks(top * INV_TEMPER + jnp.log(total))
        log_count = jnp.log(tab_ref[p].astype(F32))
        stat_ref[0, p] = segment_sum(TEMPER * (logz - log_count), qlen)
        stat_ref[1, p] = to_chunks(inv)

    top = scores(0)
    for p in range(npass):
        after = scores(p + 1) if p + 1 < npass else None
        total = powers(p, top)
        finish(p, top, total)
        top = after

    score = [stat_ref[0, k] for k in range(npass)]
    high = functools.reduce(jnp.maximum, score)
    lse = high + jnp.log(sum(jnp.exp(s - high) for s in score))
    share = [jnp.exp(s - lse) for s in score]
    hi, mid, lo = split3(lse)
    place = lax.broadcasted_iota(jnp.int32, lse.shape, 1) % qlen
    extra = jnp.where(place == 0, hi, jnp.where(place == 1, mid, lo)).astype(BF16)
    me = tab_ref[npass, :1, :1]
    own = [jnp.zeros(own_ref.shape[1:], F32) for _ in range(npass)]
    for c in range(nblk):
        part = jnp.zeros(own_ref.shape[1:], F32)
        for k in range(npass):
            g = g_ref[k, c]
            part = part + g * share[k][c : c + 1, :]
            own[k] = jnp.where(me == c, g, own[k])
        send_ref[c, :LANES, :] = part.astype(BF16)
        send_ref[c, LANES:, :] = extra
    for k in range(npass):
        own_ref[k] = own[k]


def grad_kernel(
    qlen, total, tab_ref, recv_ref, e_ref, stat_ref, own_ref, qt_ref, phid_hbm, qhid_hbm,
    qgrad_hbm, pgrad_hbm, send_ref, acc_ref, qs_ref, phid_ref, qhid_ref, qgrad_ref, pgrad_ref, sem, out_sem,
):
    nblk = qt_ref.shape[0]
    npass = stat_ref.shape[1]
    copies = [pltpu.make_async_copy(phid_hbm.at[p], phid_ref.at[p], sem.at[p]) for p in range(npass)]
    copies.append(pltpu.make_async_copy(qhid_hbm, qhid_ref, sem.at[npass]))
    for copy in copies:
        copy.start()
    me = tab_ref[npass, :1, :1]
    lane = lax.broadcasted_iota(jnp.int32, (nblk, LANES), 1)
    chunk = lax.broadcasted_iota(jnp.int32, (nblk, LANES), 0)
    mine = chunk == me

    def pick(x):
        return jnp.sum(jnp.where(mine, x, 0.0), axis=0, keepdims=True)

    parts = []
    for d in range(nblk):
        x = recv_ref[d, LANES:, :].astype(F32)
        parts.append(segment_sum(jnp.where(lane % qlen < 3, x, 0.0), qlen))
    high = functools.reduce(jnp.maximum, parts)
    lse = high + jnp.log(sum(jnp.exp(x - high) for x in parts))
    dscore = []
    loss = jnp.zeros((nblk, LANES), F32)
    for k in range(npass):
        hit = mine & (lane // qlen == k)
        dscore.append((jnp.exp(stat_ref[0, k] - lse) - hit.astype(F32)) / total)
        loss = loss + jnp.where(mine & (lane == k * qlen), lse - stat_ref[0, k], 0.0)

    grad = jnp.zeros((LANES, LANES), F32)
    for k in range(npass):
        grad = grad + own_ref[k] * pick(dscore[k])
    for d in range(nblk):
        share = jnp.where(me == d, 0.0, pick(jnp.exp(parts[d] - lse)) / total)
        grad = grad + recv_ref[d, :LANES, :].astype(F32) * share
    qgrad_ref[...] = grad.T
    outs = [pltpu.make_async_copy(qgrad_ref, qgrad_hbm, out_sem.at[npass])]
    outs[0].start()
    copies[npass].wait()
    acc_ref[...] = mm(grad.astype(BF16), qhid_ref[...], NN)


    for p in range(npass):
        weight = dscore[p] * stat_ref[1, p]
        for c in range(nblk):
            qs_ref[p % 2, :, c * LANES : (c + 1) * LANES] = (
                qt_ref[c].astype(F32) * weight[c : c + 1, :]
            ).astype(BF16)
        pgrad = mm(e_ref[p], qs_ref[p % 2], NT)
        pgrad_ref[p] = pgrad
        outs.append(pltpu.make_async_copy(pgrad_ref.at[p], pgrad_hbm.at[p], out_sem.at[p]))
        outs[-1].start()
        copies[p].wait()
        acc_ref[...] += mm(pgrad.astype(BF16), phid_ref[p], TN)
    wgrad = acc_ref[...].T

    hi, mid, lo = split3(jnp.full((1, LANES), jnp.sum(loss)))
    extra = jnp.concatenate([hi, mid, lo, jnp.zeros((5, LANES), F32)], axis=0)
    rows = send_ref.shape[1] - 8
    for r in range(send_ref.shape[0]):
        send_ref[r] = jnp.concatenate([wgrad[r * rows : (r + 1) * rows, :], extra], axis=0).astype(BF16)
    for copy in outs:
        copy.wait()


def sum_plane_kernel(x_ref, out_ref):
    y = jnp.sum(x_ref[...].astype(F32), axis=0)
    for c in range(out_ref.shape[0]):
        out_ref[c] = y


def sum_column_kernel(total, x_ref, out_ref, loss_ref):
    y = jnp.sum(x_ref[...], axis=0)
    rows = out_ref.shape[1]
    z = y[:rows].astype(BF16)
    for c in range(out_ref.shape[0]):
        out_ref[c] = z
    loss_ref[...] = jnp.broadcast_to(jnp.sum(y[rows:], axis=0, keepdims=True) / total, loss_ref.shape)


def final_kernel(x_ref, loss_in_ref, out_ref, loss_ref):
    rows = x_ref.shape[1]
    loss_ref[...] = loss_in_ref[:1, :]
    for c in range(x_ref.shape[0]):
        out_ref[c * rows : (c + 1) * rows, :] = x_ref[c].astype(F32)


VM = pl.BlockSpec(memory_space=pltpu.VMEM)
HBM = pl.BlockSpec(memory_space=pltpu.HBM)


def call(name, kernel, ins, out_shape, *args, outs=None, scratch=(), flops=0, bytes_accessed=0):
    args = [pltpu.with_memory_space_constraint(a, pltpu.HBM) if i is HBM else a for a, i in zip(args, ins)]
    return pl.pallas_call(
        kernel,
        name=name,
        out_shape=out_shape,
        in_specs=ins,
        out_specs=outs or jax.tree.map(lambda _: VM, out_shape),
        scratch_shapes=scratch,
        compiler_params=pltpu.CompilerParams(vmem_limit_bytes=32 << 20),
        cost_estimate=pl.CostEstimate(flops=flops, bytes_accessed=bytes_accessed, transcendentals=0),
    )(*args)


def shards(query_hidden, passage_hidden, lengths, projection):
    hidden, dim = projection.shape
    nquery, qlen = query_hidden.shape[1:3]
    npass, plen = passage_hidden.shape[1:3]
    nblk, nrep = lax.axis_size(BLK), lax.axis_size(REP)
    nplane, ncolumn = lax.axis_size(PLANE), lax.axis_size(COLUMN)
    total = nblk * nrep * nquery
    mine = nquery * qlen
    ntok = nblk * mine
    rows = hidden // nplane
    qflat = query_hidden[0].reshape(-1, hidden)
    S = jax.ShapeDtypeStruct

    copies = call(
        "query_tokens", query_kernel, [HBM, HBM], S((nblk, dim, mine), BF16), qflat, projection,
        scratch=[pltpu.VMEM((mine, hidden), BF16), pltpu.VMEM((hidden, dim), BF16), pltpu.SemaphoreType.DMA((2,))],
        flops=2 * mine * hidden * dim, bytes_accessed=400_000,
    )
    qt = lax.all_to_all(copies, BLK, 0, 0)
    tok, tab = call(
        "passage_tokens", passage_kernel, [HBM, HBM, HBM],
        (S((npass, 2, plen, dim), BF16), S((npass + 1, nblk, LANES), jnp.int32)),
        lengths, passage_hidden[0], projection,
        scratch=[pltpu.VMEM((npass, plen, hidden), BF16), pltpu.VMEM((hidden, dim), BF16),
                 pltpu.SMEM(lengths.shape, jnp.int32), pltpu.SemaphoreType.DMA((npass + 2,))],
        flops=2 * npass * plen * hidden * dim, bytes_accessed=8_000_000,
    )
    e, stat, send, own = call(
        "scores", functools.partial(score_kernel, qlen), [VM] * 3,
        (S((npass, plen, ntok), BF16), S((2, npass, nblk, LANES), F32), S((nblk, dim + EXTRA, LANES), BF16),
         S((npass, dim, LANES), F32)),
        qt, tok, tab,
        scratch=[pltpu.VMEM((dim, ntok), BF16), pltpu.VMEM((2, plen, ntok), F32),
                 pltpu.VMEM((npass, nblk, dim, LANES), F32)],
        flops=4 * npass * plen * ntok * dim, bytes_accessed=8_000_000,
    )
    recv = lax.all_to_all(send, BLK, 0, 0)
    qgrad, pgrad, send = call(
        "grads", functools.partial(grad_kernel, qlen, float(total)), [VM] * 6 + [HBM] * 2,
        (S((mine, dim), F32), S((npass, plen, dim), F32), S((nplane, rows + 8, dim), BF16)),
        tab, recv, e, stat, own, qt, passage_hidden[0], qflat,
        scratch=[pltpu.VMEM((dim, hidden), F32), pltpu.VMEM((2, dim, ntok), BF16), pltpu.VMEM((npass, plen, hidden), BF16),
                 pltpu.VMEM((mine, hidden), BF16), pltpu.VMEM((mine, dim), F32), pltpu.VMEM((npass, plen, dim), F32),
                 pltpu.SemaphoreType.DMA((npass + 1,)), pltpu.SemaphoreType.DMA((npass + 1,))],
        outs=(HBM, HBM, VM),
        flops=2 * npass * plen * ntok * dim, bytes_accessed=8_000_000,
    )
    part = lax.all_to_all(send, PLANE, 0, 0)
    part = call("sum_plane", sum_plane_kernel, [VM], S((ncolumn, rows + 8, dim), F32), part)
    part = lax.all_to_all(part, COLUMN, 0, 0)
    part, loss = call(
        "sum_column", functools.partial(sum_column_kernel, float(total)), [VM],
        (S((nplane, rows, dim), BF16), S((8, dim), F32)), part,
    )
    part = lax.all_to_all(part, PLANE, 0, 0)
    wgrad, loss = call("final", final_kernel, [VM, VM], (S((hidden, dim), F32), S((1, dim), F32)), part, loss)
    return (
        qgrad.reshape(1, nquery, qlen, dim),
        pgrad.reshape(1, npass, plen, dim),
        wgrad,
        loss[0, 0],
    )


def solution(mesh):
    fine = Mesh(mesh.devices.reshape(2, 4, 8, 2, 2), AXES)
    return jax.shard_map(
        shards,
        mesh=fine,
        in_specs=(P(REP, BLK, None, None), P(REP, BLK, None, None), P(REP, BLK), P()),
        out_specs=(P(REP, BLK, None, None), P(REP, BLK, None, None), P(), P()),
        check_vma=False,
    )
```

```python
import functools
import math

import jax
import jax.numpy as jnp
from jax import lax
from jax.experimental import pallas as pl
from jax.experimental.pallas import tpu as pltpu
from jax.sharding import Mesh
from jax.sharding import PartitionSpec as P

F32 = jnp.float32
BF16 = jnp.bfloat16
INV_TEMPER = 2.0
TEMPER = 0.5
EXP2_SCALE = INV_TEMPER * math.log2(math.e)
LANES = 128
EXTRA = 8
AXES = ("x_hi", "y", "z", "x_lo", "core")
BLK = ("x_hi", "y")
REP = ("z", "x_lo", "core")
PLANE = ("x_hi", "y", "x_lo", "core")
COLUMN = "z"
NN = (((1,), (0,)), ((), ()))
NT = (((1,), (1,)), ((), ()))
TN = (((0,), (0,)), ((), ()))


def mm(a, b, dims):
    return lax.dot_general(a, b, dims, preferred_element_type=F32)


def to_row(x):
    return jnp.concatenate([x[c : c + 1, :] for c in range(x.shape[0])], axis=1)


def to_chunks(x):
    n = x.shape[1] // LANES
    return jnp.concatenate([x[:, c * LANES : (c + 1) * LANES] for c in range(n)], axis=0)


def split3(x):
    hi = x.astype(BF16).astype(F32)
    rest = x - hi
    mid = rest.astype(BF16).astype(F32)
    return hi, mid, (rest - mid)


def segment_sum(x, width):
    lane = lax.broadcasted_iota(jnp.int32, x.shape, 1)
    step = 1
    while step < width:
        up = pltpu.roll(x, x.shape[1] - step, 1)
        down = pltpu.roll(x, step, 1)
        x = x + jnp.where((lane & step) == 0, up, down)
        step *= 2
    return x


def query_kernel(q_ref, w_ref, out_ref):
    tok = mm(q_ref[...], w_ref[...], NN)
    flipped = tok.T.astype(BF16)
    for c in range(out_ref.shape[0]):
        out_ref[c] = flipped


def passage_kernel(len_hbm, phid_hbm, w_hbm, tok_ref, tab_ref, phid_ref, w_ref, len_ref, sem):
    npass = phid_ref.shape[0]
    lens = pltpu.make_async_copy(len_hbm, len_ref, sem.at[npass + 1])
    lens.start()
    copies = [pltpu.make_async_copy(w_hbm, w_ref, sem.at[npass])]
    copies += [pltpu.make_async_copy(phid_hbm, phid_ref, sem.at[0])]
    for copy in copies:
        copy.start()
    shape = tab_ref.shape[1:]
    tab_ref[npass] = jnp.full(shape, lax.axis_index("x_hi") * lax.axis_size("y") + lax.axis_index("y"), jnp.int32)
    lens.wait()
    for p in range(npass):
        tab_ref[p] = jnp.full(shape, len_ref[0, p], jnp.int32)
    copies[0].wait()
    copies[1].wait()
    for p in range(npass):
        tok = mm(phid_ref[p], w_ref[...], NN)
        tok_ref[p, 0] = tok.astype(BF16)
        for r in range(0, tok.shape[0], LANES):
            tok_ref[p, 1, r : r + LANES, :] = tok[r : r + LANES, :].T.astype(BF16)


def score_kernel(
    qlen, qt_ref, tok_ref, tab_ref, phid_hbm, e_ref, stat_ref, send_ref, own_ref, phid_ref,
    qs_ref, s_ref, g_ref, sem,
):
    copies = [
        pltpu.make_async_copy(phid_hbm, phid_ref, sem.at[0]),
    ]
    for copy in copies:
        copy.start()
    nblk = qt_ref.shape[0]
    npass, slots, ntok = e_ref.shape
    for c in range(nblk):
        qs_ref[:, c * LANES : (c + 1) * LANES] = qt_ref[c]
    rows = 128

    def fold(x, op):
        return functools.reduce(op, [x[r : r + 8] for r in range(0, x.shape[0], 8)])

    def scores(p):
        top = None
        count = tab_ref[p, :1, :1]
        for r in range(0, slots, rows):
            x = mm(tok_ref[p, 0, r : r + rows, :], qs_ref[...], NN)
            row = lax.broadcasted_iota(jnp.int32, (rows, 1), 0) + r
            x = jnp.where(row < count, x, -jnp.inf)
            s_ref[p % 2, r : r + rows, :] = x
            high = fold(x, jnp.maximum)
            top = high if top is None else jnp.maximum(top, high)
        return jnp.max(top, axis=0, keepdims=True)

    def powers(p, top):
        total = jnp.zeros((8, ntok), F32)
        for r in range(0, slots, 16):
            e = jnp.exp2((s_ref[p % 2, r : r + 16, :] - top) * EXP2_SCALE)
            total = total + fold(e, jnp.add)
            e_ref[p, r : r + 16, :] = e.astype(BF16)
        return jnp.sum(total, axis=0, keepdims=True)

    def finish(p, top, total):
        inv = 1.0 / total
        flipped = jnp.concatenate([tok_ref[p, 1, r : r + LANES, :] for r in range(0, slots, LANES)], axis=1)
        g = mm(flipped, e_ref[p], NN) * inv
        for c in range(nblk):
            g_ref[p, c] = g[:, c * LANES : (c + 1) * LANES]
        logz = to_chunks(top * INV_TEMPER + jnp.log(total))
        log_count = jnp.log(tab_ref[p].astype(F32))
        stat_ref[0, p] = segment_sum(TEMPER * (logz - log_count), qlen)
        stat_ref[1, p] = to_chunks(inv)

    top = scores(0)
    for p in range(npass):
        after = scores(p + 1) if p + 1 < npass else None
        total = powers(p, top)
        finish(p, top, total)
        top = after

    score = [stat_ref[0, k] for k in range(npass)]
    high = functools.reduce(jnp.maximum, score)
    lse = high + jnp.log(sum(jnp.exp(s - high) for s in score))
    share = [jnp.exp(s - lse) for s in score]
    hi, mid, lo = split3(lse)
    place = lax.broadcasted_iota(jnp.int32, lse.shape, 1) % 4
    extra = jnp.where(place == 0, hi, jnp.where(place == 1, mid, jnp.where(place == 2, lo, 0.0))).astype(BF16)
    me = tab_ref[npass, :1, :1]
    own = [jnp.zeros(own_ref.shape[1:], F32) for _ in range(npass)]
    for c in range(nblk):
        part = jnp.zeros(own_ref.shape[1:], F32)
        for k in range(npass):
            g = g_ref[k, c]
            part = part + g * share[k][c : c + 1, :]
            own[k] = jnp.where(me == c, g, own[k])
        send_ref[c, :LANES, :] = part.astype(BF16)
        send_ref[c, LANES:, :] = extra
    for k in range(npass):
        own_ref[k] = own[k]
    for copy in copies:
        copy.wait()


def grad_kernel(
    qlen, total, tab_ref, recv_ref, e_ref, stat_ref, own_ref, qt_ref, phid_ref, qhid_ref,
    qgrad_ref, pgrad_ref, send_ref, acc_ref, qs_ref,
):
    nblk = qt_ref.shape[0]
    npass = stat_ref.shape[1]
    me = tab_ref[npass, :1, :1]
    lane = lax.broadcasted_iota(jnp.int32, (nblk, LANES), 1)
    chunk = lax.broadcasted_iota(jnp.int32, (nblk, LANES), 0)
    mine = chunk == me

    def pick(x):
        return jnp.sum(jnp.where(mine, x, 0.0), axis=0, keepdims=True)

    parts = []
    for d in range(nblk):
        parts.append(segment_sum(recv_ref[d, LANES:, :].astype(F32), 4))
    high = functools.reduce(jnp.maximum, parts)
    lse = high + jnp.log(sum(jnp.exp(x - high) for x in parts))
    dscore = []
    loss = jnp.zeros((nblk, LANES), F32)
    for k in range(npass):
        hit = mine & (lane // qlen == k)
        dscore.append((jnp.exp(stat_ref[0, k] - lse) - hit.astype(F32)) / total)
        loss = loss + jnp.where(mine & (lane == k * qlen), lse - stat_ref[0, k], 0.0)

    for p in range(npass):
        weight = dscore[p] * stat_ref[1, p]
        for c in range(nblk):
            qs_ref[p % 2, :, c * LANES : (c + 1) * LANES] = (
                qt_ref[c].astype(F32) * weight[c : c + 1, :]
            ).astype(BF16)
        pgrad = mm(e_ref[p], qs_ref[p % 2], NT)
        pgrad_ref[p] = pgrad
        term = mm(pgrad.astype(BF16), phid_ref[p], TN)
        acc_ref[...] = term if p == 0 else acc_ref[...] + term
    grad = jnp.zeros((LANES, LANES), F32)
    for k in range(npass):
        grad = grad + own_ref[k] * pick(dscore[k])
    for d in range(nblk):
        share = jnp.where(me == d, 0.0, pick(jnp.exp(parts[d] - lse)) / total)
        grad = grad + recv_ref[d, :LANES, :].astype(F32) * share
    qgrad_ref[...] = grad.T
    wgrad = (acc_ref[...] + mm(grad.astype(BF16), qhid_ref[...], NN)).T


    hi, mid, lo = split3(jnp.full((1, LANES), jnp.sum(loss)))
    extra = jnp.concatenate([hi, mid, lo, jnp.zeros((5, LANES), F32)], axis=0)
    rows = send_ref.shape[1] - 8
    for r in range(send_ref.shape[0]):
        send_ref[r] = jnp.concatenate([wgrad[r * rows : (r + 1) * rows, :], extra], axis=0).astype(BF16)


def sum_plane_kernel(x_ref, out_ref):
    y = jnp.sum(x_ref[...].astype(F32), axis=0)
    for c in range(out_ref.shape[0]):
        out_ref[c] = y


def sum_column_kernel(total, x_ref, out_ref, loss_ref):
    y = jnp.sum(x_ref[...], axis=0)
    rows = out_ref.shape[1]
    z = y[:rows].astype(BF16)
    for c in range(out_ref.shape[0]):
        out_ref[c] = z
    loss_ref[...] = jnp.broadcast_to(jnp.sum(y[rows:], axis=0, keepdims=True) / total, loss_ref.shape)


def final_kernel(x_ref, loss_in_ref, out_ref, loss_ref):
    rows = x_ref.shape[1]
    loss_ref[...] = loss_in_ref[:1, :]
    for c in range(x_ref.shape[0]):
        out_ref[c * rows : (c + 1) * rows, :] = x_ref[c].astype(F32)


VM = pl.BlockSpec(memory_space=pltpu.VMEM)
HBM = pl.BlockSpec(memory_space=pltpu.HBM)
FAR = pl.BlockSpec(memory_space=pltpu.VMEM)


def call(name, kernel, ins, out_shape, *args, outs=None, scratch=(), flops=0, bytes_accessed=0):
    args = [pltpu.with_memory_space_constraint(a, pltpu.HBM) if i is HBM or i is FAR else a for a, i in zip(args, ins)]
    return pl.pallas_call(
        kernel,
        name=name,
        out_shape=out_shape,
        in_specs=ins,
        out_specs=outs or jax.tree.map(lambda _: VM, out_shape),
        scratch_shapes=scratch,
        compiler_params=pltpu.CompilerParams(vmem_limit_bytes=32 << 20),
        cost_estimate=pl.CostEstimate(flops=flops, bytes_accessed=bytes_accessed, transcendentals=0),
    )(*args)


def query_call(qhid, projection, nblk):
    mine, hidden = qhid.shape
    dim = projection.shape[1]
    return call(
        "query_tokens", query_kernel, [FAR, FAR], pltpu.VMEM((nblk, dim, mine), BF16), qhid, projection,
        flops=2 * mine * hidden * dim, bytes_accessed=400_000,
    )


def passage_call(lengths, phid, projection, nblk):
    npass, plen, hidden = phid.shape
    dim = projection.shape[1]
    S = jax.ShapeDtypeStruct
    return call(
        "passage_tokens", passage_kernel, [HBM, HBM, HBM],
        (S((npass, 2, plen, dim), BF16), S((npass + 1, nblk, LANES), jnp.int32)),
        lengths, phid, projection,
        scratch=[pltpu.VMEM((npass, plen, hidden), BF16), pltpu.VMEM((hidden, dim), BF16),
                 pltpu.SMEM(lengths.shape, jnp.int32), pltpu.SemaphoreType.DMA((npass + 2,))],
        flops=2 * npass * plen * hidden * dim, bytes_accessed=8_000_000,
    )


def score_call(qt, tok, tab, phid, qlen):
    nblk, dim, _ = qt.shape
    npass, _, plen, _ = tok.shape
    ntok = nblk * LANES
    S = jax.ShapeDtypeStruct
    return call(
        "scores", functools.partial(score_kernel, qlen), [VM] * 3 + [HBM],
        (S((npass, plen, ntok), BF16), S((2, npass, nblk, LANES), F32), S((nblk, dim + EXTRA, LANES), BF16),
         S((npass, dim, LANES), F32), S(phid.shape, BF16)),
        qt, tok, tab, phid,
        scratch=[pltpu.VMEM((dim, ntok), BF16), pltpu.VMEM((2, plen, ntok), F32),
                 pltpu.VMEM((npass, nblk, dim, LANES), F32), pltpu.SemaphoreType.DMA((2,))],
        flops=4 * npass * plen * ntok * dim, bytes_accessed=8_000_000,
    )


def grad_call(tab, recv, e, stat, own, qt, phid, qhid, qlen, total, nplane):
    npass, plen, ntok = e.shape
    mine, hidden = qhid.shape
    dim = qt.shape[1]
    rows = hidden // nplane
    S = jax.ShapeDtypeStruct
    return call(
        "grads", functools.partial(grad_kernel, qlen, total), [VM] * 8,
        (S((mine, dim), F32), S((npass, plen, dim), F32), S((nplane, rows + 8, dim), BF16)),
        tab, recv, e, stat, own, qt, phid, qhid,
        scratch=[pltpu.VMEM((dim, hidden), F32), pltpu.VMEM((2, dim, ntok), BF16)],
        flops=2 * npass * plen * ntok * dim, bytes_accessed=8_000_000,
    )


def shards(query_hidden, passage_hidden, lengths, projection):
    hidden, dim = projection.shape
    nquery, qlen = query_hidden.shape[1:3]
    npass, plen = passage_hidden.shape[1:3]
    nblk, nrep = lax.axis_size(BLK), lax.axis_size(REP)
    nplane, ncolumn = lax.axis_size(PLANE), lax.axis_size(COLUMN)
    total = nblk * nrep * nquery
    mine = nquery * qlen
    ntok = nblk * mine
    rows = hidden // nplane
    qflat = query_hidden[0].reshape(-1, hidden)
    S = jax.ShapeDtypeStruct

    copies = query_call(qflat, projection, nblk)
    qt = lax.all_to_all(copies, BLK, 0, 0)
    tok, tab = passage_call(lengths, passage_hidden[0], projection, nblk)
    e, stat, send, own, phid = score_call(qt, tok, tab, passage_hidden[0], qlen)
    recv = lax.all_to_all(send, BLK, 0, 0)
    qgrad, pgrad, send = grad_call(tab, recv, e, stat, own, qt, phid, qflat, qlen, float(total), nplane)
    part = lax.all_to_all(send, PLANE, 0, 0)
    part = call("sum_plane", sum_plane_kernel, [VM], S((ncolumn, rows + 8, dim), F32), part)
    part = lax.all_to_all(part, COLUMN, 0, 0)
    part, loss = call(
        "sum_column", functools.partial(sum_column_kernel, float(total)), [VM],
        (S((nplane, rows, dim), BF16), S((8, dim), F32)), part,
    )
    part = lax.all_to_all(part, PLANE, 0, 0)
    wgrad, loss = call("final", final_kernel, [VM, VM], (S((hidden, dim), F32), S((1, dim), F32)), part, loss)
    return (
        qgrad.reshape(1, nquery, qlen, dim),
        pgrad.reshape(1, npass, plen, dim),
        wgrad,
        loss[0, 0],
    )


def solution(mesh):
    fine = Mesh(mesh.devices.reshape(2, 4, 8, 2, 2), AXES)
    return jax.shard_map(
        shards,
        mesh=fine,
        in_specs=(P(REP, BLK, None, None), P(REP, BLK, None, None), P(REP, BLK), P()),
        out_specs=(P(REP, BLK, None, None), P(REP, BLK, None, None), P(), P()),
        check_vma=False,
    )
```

```python
import functools
import math

import jax
import jax.numpy as jnp
from jax import lax
from jax.experimental import pallas as pl
from jax.experimental.pallas import tpu as pltpu
from jax.sharding import Mesh
from jax.sharding import PartitionSpec as P

F32 = jnp.float32
BF16 = jnp.bfloat16
INV_TEMPER = 2.0
TEMPER = 0.5
EXP2_SCALE = INV_TEMPER * math.log2(math.e)
LANES = 128
EXTRA = 8
AXES = ("x_hi", "y", "z", "x_lo", "core")
BLK = ("x_hi", "y")
REP = ("z", "x_lo", "core")
PLANE = ("x_hi", "y", "x_lo")
COLUMN = "z"
NN = (((1,), (0,)), ((), ()))
NT = (((1,), (1,)), ((), ()))
TN = (((0,), (0,)), ((), ()))


def mm(a, b, dims):
    return lax.dot_general(a, b, dims, preferred_element_type=F32)


def to_row(x):
    return jnp.concatenate([x[c : c + 1, :] for c in range(x.shape[0])], axis=1)


def to_chunks(x):
    n = x.shape[1] // LANES
    return jnp.concatenate([x[:, c * LANES : (c + 1) * LANES] for c in range(n)], axis=0)


def split3(x):
    hi = x.astype(BF16).astype(F32)
    rest = x - hi
    mid = rest.astype(BF16).astype(F32)
    return hi, mid, (rest - mid)


def segment_sum(x, width):
    lane = lax.broadcasted_iota(jnp.int32, x.shape, 1)
    step = 1
    while step < width:
        up = pltpu.roll(x, x.shape[1] - step, 1)
        down = pltpu.roll(x, step, 1)
        x = x + jnp.where((lane & step) == 0, up, down)
        step *= 2
    return x


def query_kernel(q_ref, w_ref, out_ref):
    tok = mm(q_ref[...], w_ref[...], NN)
    flipped = tok.T.astype(BF16)
    for c in range(out_ref.shape[0]):
        out_ref[c] = flipped


def passage_kernel(len_hbm, phid_hbm, w_hbm, tok_ref, tab_ref, phid_ref, w_ref, len_ref, sem):
    npass = phid_ref.shape[0]
    lens = pltpu.make_async_copy(len_hbm, len_ref, sem.at[npass + 1])
    lens.start()
    copies = [pltpu.make_async_copy(w_hbm, w_ref, sem.at[npass])]
    half = npass // 2
    for k, at in enumerate((pl.ds(0, half), pl.ds(half, npass - half))):
        copies.append(pltpu.make_async_copy(phid_hbm.at[at], phid_ref.at[at], sem.at[k]))
    for copy in copies:
        copy.start()
    shape = tab_ref.shape[1:]
    tab_ref[npass] = jnp.full(shape, lax.axis_index("x_hi") * lax.axis_size("y") + lax.axis_index("y"), jnp.int32)
    lens.wait()
    for p in range(npass):
        tab_ref[p] = jnp.full(shape, len_ref[0, p], jnp.int32)
    copies[0].wait()
    for p in range(npass):
        if p == 0:
            copies[1].wait()
        if p == half:
            copies[2].wait()
        tok = mm(phid_ref[p], w_ref[...], NN)
        tok_ref[p, 0] = tok.astype(BF16)
        for r in range(0, tok.shape[0], LANES):
            tok_ref[p, 1, r : r + LANES, :] = tok[r : r + LANES, :].T.astype(BF16)


def score_kernel(
    qlen, qt_ref, tok_ref, tab_ref, phid_hbm, e_ref, stat_ref, send_ref, own_ref, phid_ref,
    qs_ref, s_ref, g_ref, sem,
):
    copies = [
        pltpu.make_async_copy(phid_hbm, phid_ref, sem.at[0]),
    ]
    for copy in copies:
        copy.start()
    nblk = qt_ref.shape[0]
    npass, slots, ntok = e_ref.shape
    for c in range(nblk):
        qs_ref[:, c * LANES : (c + 1) * LANES] = qt_ref[c]
    rows = 128

    def fold(x, op):
        return functools.reduce(op, [x[r : r + 8] for r in range(0, x.shape[0], 8)])

    def scores(p):
        top = None
        count = tab_ref[p, :1, :1]
        for r in range(0, slots, rows):
            x = mm(tok_ref[p, 0, r : r + rows, :], qs_ref[...], NN)
            row = lax.broadcasted_iota(jnp.int32, (rows, 1), 0) + r
            x = jnp.where(row < count, x, -jnp.inf)
            s_ref[p % 2, r : r + rows, :] = x
            high = fold(x, jnp.maximum)
            top = high if top is None else jnp.maximum(top, high)
        return jnp.max(top, axis=0, keepdims=True)

    def powers(p, top):
        total = jnp.zeros((8, ntok), F32)
        for r in range(0, slots, 16):
            e = jnp.exp2((s_ref[p % 2, r : r + 16, :] - top) * EXP2_SCALE)
            total = total + fold(e, jnp.add)
            e_ref[p, r : r + 16, :] = e.astype(BF16)
        return jnp.sum(total, axis=0, keepdims=True)

    def finish(p, top, total):
        inv = 1.0 / total
        flipped = jnp.concatenate([tok_ref[p, 1, r : r + LANES, :] for r in range(0, slots, LANES)], axis=1)
        g = mm(flipped, e_ref[p], NN) * inv
        for c in range(nblk):
            g_ref[p, c] = g[:, c * LANES : (c + 1) * LANES]
        logz = to_chunks(top * INV_TEMPER + jnp.log(total))
        log_count = jnp.log(tab_ref[p].astype(F32))
        stat_ref[0, p] = segment_sum(TEMPER * (logz - log_count), qlen)
        stat_ref[1, p] = to_chunks(inv)

    top = scores(0)
    for p in range(npass):
        after = scores(p + 1) if p + 1 < npass else None
        total = powers(p, top)
        finish(p, top, total)
        top = after

    score = [stat_ref[0, k] for k in range(npass)]
    high = functools.reduce(jnp.maximum, score)
    lse = high + jnp.log(sum(jnp.exp(s - high) for s in score))
    share = [jnp.exp(s - lse) for s in score]
    hi, mid, lo = split3(lse)
    place = lax.broadcasted_iota(jnp.int32, lse.shape, 1) % 4
    extra = jnp.where(place == 0, hi, jnp.where(place == 1, mid, jnp.where(place == 2, lo, 0.0))).astype(BF16)
    me = tab_ref[npass, :1, :1]
    own = [jnp.zeros(own_ref.shape[1:], F32) for _ in range(npass)]
    for c in range(nblk):
        part = jnp.zeros(own_ref.shape[1:], F32)
        for k in range(npass):
            g = g_ref[k, c]
            part = part + g * share[k][c : c + 1, :]
            own[k] = jnp.where(me == c, g, own[k])
        send_ref[c, :LANES, :] = part.astype(BF16)
        send_ref[c, LANES:, :] = extra
    for k in range(npass):
        own_ref[k] = own[k]
    for copy in copies:
        copy.wait()


def grad_kernel(
    qlen, total, tab_ref, recv_ref, e_ref, stat_ref, own_ref, qt_ref, phid_ref, qhid_ref,
    qgrad_ref, pgrad_ref, send_ref, acc_ref, qs_ref, small_ref,
):
    nblk = qt_ref.shape[0]
    npass = stat_ref.shape[1]
    me = tab_ref[npass, :1, :1]
    lane = lax.broadcasted_iota(jnp.int32, (nblk, LANES), 1)
    chunk = lax.broadcasted_iota(jnp.int32, (nblk, LANES), 0)
    mine = chunk == me

    def pick(x):
        return jnp.sum(jnp.where(mine, x, 0.0), axis=0, keepdims=True)

    parts = []
    for d in range(nblk):
        parts.append(segment_sum(recv_ref[d, LANES:, :].astype(F32), 4))
    high = functools.reduce(jnp.maximum, parts)
    lse = high + jnp.log(sum(jnp.exp(x - high) for x in parts))
    dscore = []
    loss = jnp.zeros((nblk, LANES), F32)
    for k in range(npass):
        hit = mine & (lane // qlen == k)
        dscore.append((jnp.exp(stat_ref[0, k] - lse) - hit.astype(F32)) / total)
        loss = loss + jnp.where(mine & (lane == k * qlen), lse - stat_ref[0, k], 0.0)

    for p in range(npass):
        weight = dscore[p] * stat_ref[1, p]
        for c in range(nblk):
            qs_ref[p % 2, :, c * LANES : (c + 1) * LANES] = (
                qt_ref[c].astype(F32) * weight[c : c + 1, :]
            ).astype(BF16)
        pgrad = mm(e_ref[p], qs_ref[p % 2], NT)
        pgrad_ref[p] = pgrad
        small_ref[p * pgrad.shape[0] : (p + 1) * pgrad.shape[0], :] = pgrad.astype(BF16)
    acc_ref[...] = mm(small_ref[...], phid_ref[...].reshape(small_ref.shape[0], -1), TN)
    grad = jnp.zeros((LANES, LANES), F32)
    for k in range(npass):
        grad = grad + own_ref[k] * pick(dscore[k])
    for d in range(nblk):
        share = jnp.where(me == d, 0.0, pick(jnp.exp(parts[d] - lse)) / total)
        grad = grad + recv_ref[d, :LANES, :].astype(F32) * share
    qgrad_ref[...] = grad.T
    wgrad = (acc_ref[...] + mm(grad.astype(BF16), qhid_ref[...], NN)).T


    hi, mid, lo = split3(jnp.full((1, LANES), jnp.sum(loss)))
    extra = jnp.concatenate([hi, mid, lo, jnp.zeros((5, LANES), F32)], axis=0)
    rows = send_ref.shape[1] - 8
    for r in range(send_ref.shape[0]):
        send_ref[r] = jnp.concatenate([wgrad[r * rows : (r + 1) * rows, :], extra], axis=0).astype(BF16)


def sum_plane_kernel(x_ref, out_ref):
    out_ref[...] = jnp.sum(x_ref[...].astype(F32), axis=0)


def sum_pair_kernel(x_ref, y_ref, out_ref):
    y = x_ref[...] + y_ref[...]
    rows = y.shape[0] - 8
    hi, mid, lo = split3(jnp.sum(y[rows:], axis=0, keepdims=True))
    y = jnp.concatenate([y[:rows], hi, mid, lo, jnp.zeros((5, LANES), F32)], axis=0).astype(BF16)
    for c in range(out_ref.shape[0]):
        out_ref[c] = y


def sum_column_kernel(total, x_ref, out_ref, loss_ref):
    y = jnp.sum(x_ref[...].astype(F32), axis=0)
    rows = out_ref.shape[1]
    z = y[:rows].astype(BF16)
    for c in range(out_ref.shape[0]):
        out_ref[c] = z
    loss_ref[...] = jnp.broadcast_to(jnp.sum(y[rows:], axis=0, keepdims=True) / total, loss_ref.shape)


def final_kernel(x_ref, loss_in_ref, out_ref, loss_ref):
    rows = x_ref.shape[1]
    loss_ref[...] = loss_in_ref[:1, :]
    for c in range(x_ref.shape[0]):
        out_ref[c * rows : (c + 1) * rows, :] = x_ref[c].astype(F32)


VM = pl.BlockSpec(memory_space=pltpu.VMEM)
HBM = pl.BlockSpec(memory_space=pltpu.HBM)
FAR = pl.BlockSpec(memory_space=pltpu.VMEM)


def call(name, kernel, ins, out_shape, *args, outs=None, scratch=(), flops=0, bytes_accessed=0):
    args = [pltpu.with_memory_space_constraint(a, pltpu.HBM) if i is HBM or i is FAR else a for a, i in zip(args, ins)]
    return pl.pallas_call(
        kernel,
        name=name,
        out_shape=out_shape,
        in_specs=ins,
        out_specs=outs or jax.tree.map(lambda _: VM, out_shape),
        scratch_shapes=scratch,
        compiler_params=pltpu.CompilerParams(vmem_limit_bytes=32 << 20),
        cost_estimate=pl.CostEstimate(flops=flops, bytes_accessed=bytes_accessed, transcendentals=0),
    )(*args)


def query_call(qhid, projection, nblk):
    mine, hidden = qhid.shape
    dim = projection.shape[1]
    return call(
        "query_tokens", query_kernel, [FAR, FAR], pltpu.VMEM((nblk, dim, mine), BF16), qhid, projection,
        flops=2 * mine * hidden * dim, bytes_accessed=400_000,
    )


def passage_call(lengths, phid, projection, nblk):
    npass, plen, hidden = phid.shape
    dim = projection.shape[1]
    S = jax.ShapeDtypeStruct
    return call(
        "passage_tokens", passage_kernel, [HBM, HBM, HBM],
        (S((npass, 2, plen, dim), BF16), S((npass + 1, nblk, LANES), jnp.int32)),
        lengths, phid, projection,
        scratch=[pltpu.VMEM((npass, plen, hidden), BF16), pltpu.VMEM((hidden, dim), BF16),
                 pltpu.SMEM(lengths.shape, jnp.int32), pltpu.SemaphoreType.DMA((npass + 2,))],
        flops=2 * npass * plen * hidden * dim, bytes_accessed=8_000_000,
    )


def score_call(qt, tok, tab, phid, qlen):
    nblk, dim, _ = qt.shape
    npass, _, plen, _ = tok.shape
    ntok = nblk * LANES
    S = jax.ShapeDtypeStruct
    return call(
        "scores", functools.partial(score_kernel, qlen), [VM] * 3 + [HBM],
        (S((npass, plen, ntok), BF16), S((2, npass, nblk, LANES), F32), S((nblk, dim + EXTRA, LANES), BF16),
         S((npass, dim, LANES), F32), S(phid.shape, BF16)),
        qt, tok, tab, phid,
        scratch=[pltpu.VMEM((dim, ntok), BF16), pltpu.VMEM((2, plen, ntok), F32),
                 pltpu.VMEM((npass, nblk, dim, LANES), F32), pltpu.SemaphoreType.DMA((2,))],
        flops=4 * npass * plen * ntok * dim, bytes_accessed=8_000_000,
    )


def grad_call(tab, recv, e, stat, own, qt, phid, qhid, qlen, total, nplane):
    npass, plen, ntok = e.shape
    mine, hidden = qhid.shape
    dim = qt.shape[1]
    rows = hidden // nplane
    S = jax.ShapeDtypeStruct
    return call(
        "grads", functools.partial(grad_kernel, qlen, total), [VM] * 8,
        (S((mine, dim), F32), S((npass, plen, dim), F32), S((nplane, rows + 8, dim), BF16)),
        tab, recv, e, stat, own, qt, phid, qhid,
        scratch=[pltpu.VMEM((dim, hidden), F32), pltpu.VMEM((2, dim, ntok), BF16), pltpu.VMEM((npass * plen, dim), BF16)],
        flops=2 * npass * plen * ntok * dim, bytes_accessed=8_000_000,
    )


def shards(query_hidden, passage_hidden, lengths, projection):
    hidden, dim = projection.shape
    nquery, qlen = query_hidden.shape[1:3]
    npass, plen = passage_hidden.shape[1:3]
    nblk, nrep = lax.axis_size(BLK), lax.axis_size(REP)
    nplane, ncolumn = lax.axis_size(PLANE), lax.axis_size(COLUMN)
    total = nblk * nrep * nquery
    mine = nquery * qlen
    ntok = nblk * mine
    rows = hidden // nplane
    qflat = query_hidden[0].reshape(-1, hidden)
    S = jax.ShapeDtypeStruct

    copies = query_call(qflat, projection, nblk)
    qt = lax.all_to_all(copies, BLK, 0, 0)
    tok, tab = passage_call(lengths, passage_hidden[0], projection, nblk)
    e, stat, send, own, phid = score_call(qt, tok, tab, passage_hidden[0], qlen)
    recv = lax.all_to_all(send, BLK, 0, 0)
    qgrad, pgrad, send = grad_call(tab, recv, e, stat, own, qt, phid, qflat, qlen, float(total), nplane)
    part = lax.all_to_all(send, PLANE, 0, 0)
    part = call("sum_plane", sum_plane_kernel, [VM], S((rows + 8, dim), F32), part)
    twin = lax.ppermute(part, "core", [(0, 1), (1, 0)])
    part = call("sum_pair", sum_pair_kernel, [VM, VM], S((ncolumn, rows + 8, dim), BF16), part, twin)
    part = lax.all_to_all(part, COLUMN, 0, 0)
    part, loss = call(
        "sum_column", functools.partial(sum_column_kernel, float(total)), [VM],
        (S((nplane, rows, dim), BF16), S((8, dim), F32)), part,
    )
    part = lax.all_to_all(part, PLANE, 0, 0)
    wgrad, loss = call("final", final_kernel, [VM, VM], (S((hidden, dim), F32), S((1, dim), F32)), part, loss)
    return (
        qgrad.reshape(1, nquery, qlen, dim),
        pgrad.reshape(1, npass, plen, dim),
        wgrad,
        loss[0, 0],
    )


def solution(mesh):
    fine = Mesh(mesh.devices.reshape(2, 4, 8, 2, 2), AXES)
    return jax.shard_map(
        shards,
        mesh=fine,
        in_specs=(P(REP, BLK, None, None), P(REP, BLK, None, None), P(REP, BLK), P()),
        out_specs=(P(REP, BLK, None, None), P(REP, BLK, None, None), P(), P()),
        check_vma=False,
    )
```

```python
import functools
import math

import jax
import jax.numpy as jnp
from jax import lax
from jax.experimental import pallas as pl
from jax.experimental.pallas import tpu as pltpu
from jax.sharding import Mesh
from jax.sharding import PartitionSpec as P

F32 = jnp.float32
BF16 = jnp.bfloat16
INV_TEMPER = 2.0
TEMPER = 0.5
EXP2_SCALE = INV_TEMPER * math.log2(math.e)
LANES = 128
EXTRA = 8
AXES = ("x_hi", "y", "z", "x_lo", "core")
BLK = ("x_hi", "y")
REP = ("z", "x_lo", "core")
PLANE = ("x_hi", "y", "x_lo")
COLUMN = "z"
NN = (((1,), (0,)), ((), ()))
NT = (((1,), (1,)), ((), ()))
TN = (((0,), (0,)), ((), ()))


def mm(a, b, dims):
    return lax.dot_general(a, b, dims, preferred_element_type=F32)


def to_row(x):
    return jnp.concatenate([x[c : c + 1, :] for c in range(x.shape[0])], axis=1)


def to_chunks(x):
    n = x.shape[1] // LANES
    return jnp.concatenate([x[:, c * LANES : (c + 1) * LANES] for c in range(n)], axis=0)


def split3(x):
    hi = x.astype(BF16).astype(F32)
    rest = x - hi
    mid = rest.astype(BF16).astype(F32)
    return hi, mid, (rest - mid)


def segment_sum(x, width):
    lane = lax.broadcasted_iota(jnp.int32, x.shape, 1)
    step = 1
    while step < width:
        up = pltpu.roll(x, x.shape[1] - step, 1)
        down = pltpu.roll(x, step, 1)
        x = x + jnp.where((lane & step) == 0, up, down)
        step *= 2
    return x


def query_kernel(q_ref, w_ref, out_ref):
    tok = mm(q_ref[...], w_ref[...], NN)
    flipped = tok.T.astype(BF16)
    for c in range(out_ref.shape[0]):
        out_ref[c] = flipped


def passage_kernel(len_hbm, phid_hbm, w_hbm, tok_ref, tab_ref, phid_ref, w_ref, len_ref, sem):
    npass = phid_ref.shape[0]
    lens = pltpu.make_async_copy(len_hbm, len_ref, sem.at[npass + 1])
    lens.start()
    copies = [pltpu.make_async_copy(w_hbm, w_ref, sem.at[npass])]
    half = npass // 2
    for k, at in enumerate((pl.ds(0, half), pl.ds(half, npass - half))):
        copies.append(pltpu.make_async_copy(phid_hbm.at[at], phid_ref.at[at], sem.at[k]))
    for copy in copies:
        copy.start()
    shape = tab_ref.shape[1:]
    tab_ref[npass] = jnp.full(shape, lax.axis_index("x_hi") * lax.axis_size("y") + lax.axis_index("y"), jnp.int32)
    lens.wait()
    for p in range(npass):
        tab_ref[p] = jnp.full(shape, len_ref[0, p], jnp.int32)
    copies[0].wait()
    for p in range(npass):
        if p == 0:
            copies[1].wait()
        if p == half:
            copies[2].wait()
        tok = mm(phid_ref[p], w_ref[...], NN)
        tok_ref[p, 0] = tok.astype(BF16)
        for r in range(0, tok.shape[0], LANES):
            tok_ref[p, 1, r : r + LANES, :] = tok[r : r + LANES, :].T.astype(BF16)


def score_kernel(
    qlen, qt_ref, tok_ref, tab_ref, phid_hbm, e_ref, stat_ref, send_ref, own_ref, phid_ref,
    qs_ref, s_ref, g_ref, top_ref, sem,
):
    copies = [
        pltpu.make_async_copy(phid_hbm, phid_ref, sem.at[0]),
    ]
    for copy in copies:
        copy.start()
    nblk = qt_ref.shape[0]
    npass, slots, ntok = e_ref.shape
    for c in range(nblk):
        qs_ref[:, c * LANES : (c + 1) * LANES] = qt_ref[c]
    rows = 128

    def fold(x, op):
        return functools.reduce(op, [x[r : r + 8] for r in range(0, x.shape[0], 8)])

    def scores(p):
        top = None
        count = tab_ref[p, :1, :1]
        for r in range(0, slots, rows):
            x = mm(tok_ref[p, 0, r : r + rows, :], qs_ref[...], NN)
            row = lax.broadcasted_iota(jnp.int32, (rows, 1), 0) + r
            x = jnp.where(row < count, x, -jnp.inf)
            s_ref[p % 2, r : r + rows, :] = x
            high = fold(x, jnp.maximum)
            top = high if top is None else jnp.maximum(top, high)
        return jnp.max(top, axis=0, keepdims=True)

    def powers(p, top):
        total = jnp.zeros((8, ntok), F32)
        top_ref[...] = jnp.broadcast_to(top, (8, ntok))
        wide = top_ref[...]
        for r in range(0, slots, 16):
            parts = [jnp.exp2((s_ref[p % 2, q : q + 8, :] - wide) * EXP2_SCALE) for q in (r, r + 8)]
            total = total + (parts[0] + parts[1])
            e_ref[p, r : r + 16, :] = jnp.concatenate(parts, axis=0).astype(BF16)
        return jnp.sum(total, axis=0, keepdims=True)

    def finish(p, top, total):
        inv = 1.0 / total
        flipped = jnp.concatenate([tok_ref[p, 1, r : r + LANES, :] for r in range(0, slots, LANES)], axis=1)
        g = mm(flipped, e_ref[p], NN) * inv
        for c in range(nblk):
            g_ref[p, c] = g[:, c * LANES : (c + 1) * LANES]
        logz = to_chunks(top * INV_TEMPER + jnp.log(total))
        log_count = jnp.log(tab_ref[p].astype(F32))
        stat_ref[0, p] = segment_sum(TEMPER * (logz - log_count), qlen)
        stat_ref[1, p] = to_chunks(inv)

    top = scores(0)
    for p in range(npass):
        after = scores(p + 1) if p + 1 < npass else None
        total = powers(p, top)
        finish(p, top, total)
        top = after

    score = [stat_ref[0, k] for k in range(npass)]
    high = functools.reduce(jnp.maximum, score)
    lse = high + jnp.log(sum(jnp.exp(s - high) for s in score))
    share = [jnp.exp(s - lse) for s in score]
    hi, mid, lo = split3(lse)
    place = lax.broadcasted_iota(jnp.int32, lse.shape, 1) % 4
    extra = jnp.where(place == 0, hi, jnp.where(place == 1, mid, jnp.where(place == 2, lo, 0.0))).astype(BF16)
    me = tab_ref[npass, :1, :1]
    own = [jnp.zeros(own_ref.shape[1:], F32) for _ in range(npass)]
    for c in range(nblk):
        part = jnp.zeros(own_ref.shape[1:], F32)
        for k in range(npass):
            g = g_ref[k, c]
            part = part + g * share[k][c : c + 1, :]
            own[k] = jnp.where(me == c, g, own[k])
        send_ref[c, :LANES, :] = part.astype(BF16)
        send_ref[c, LANES:, :] = extra
    for k in range(npass):
        own_ref[k] = own[k]
    for copy in copies:
        copy.wait()


def grad_kernel(
    qlen, total, tab_ref, recv_ref, e_ref, stat_ref, own_ref, qt_ref, phid_ref, qhid_ref,
    qgrad_ref, pgrad_ref, send_ref, acc_ref, qs_ref, small_ref,
):
    nblk = qt_ref.shape[0]
    npass = stat_ref.shape[1]
    me = tab_ref[npass, :1, :1]
    lane = lax.broadcasted_iota(jnp.int32, (nblk, LANES), 1)
    chunk = lax.broadcasted_iota(jnp.int32, (nblk, LANES), 0)
    mine = chunk == me

    def pick(x):
        return jnp.sum(jnp.where(mine, x, 0.0), axis=0, keepdims=True)

    parts = []
    for d in range(nblk):
        parts.append(segment_sum(recv_ref[d, LANES:, :].astype(F32), 4))
    high = functools.reduce(jnp.maximum, parts)
    lse = high + jnp.log(sum(jnp.exp(x - high) for x in parts))
    dscore = []
    loss = jnp.zeros((nblk, LANES), F32)
    for k in range(npass):
        hit = mine & (lane // qlen == k)
        dscore.append((jnp.exp(stat_ref[0, k] - lse) - hit.astype(F32)) / total)
        loss = loss + jnp.where(mine & (lane == k * qlen), lse - stat_ref[0, k], 0.0)

    for p in range(npass):
        weight = dscore[p] * stat_ref[1, p]
        for c in range(nblk):
            qs_ref[p % 2, :, c * LANES : (c + 1) * LANES] = (
                qt_ref[c].astype(F32) * weight[c : c + 1, :]
            ).astype(BF16)
        pgrad = mm(e_ref[p], qs_ref[p % 2], NT)
        pgrad_ref[p] = pgrad
        small_ref[p * pgrad.shape[0] : (p + 1) * pgrad.shape[0], :] = pgrad.astype(BF16)
    acc_ref[...] = mm(small_ref[...], phid_ref[...].reshape(small_ref.shape[0], -1), TN)
    grad = jnp.zeros((LANES, LANES), F32)
    for k in range(npass):
        grad = grad + own_ref[k] * pick(dscore[k])
    for d in range(nblk):
        share = jnp.where(me == d, 0.0, pick(jnp.exp(parts[d] - lse)) / total)
        grad = grad + recv_ref[d, :LANES, :].astype(F32) * share
    qgrad_ref[...] = grad.T
    wgrad = (acc_ref[...] + mm(grad.astype(BF16), qhid_ref[...], NN)).T


    hi, mid, lo = split3(jnp.full((1, LANES), jnp.sum(loss)))
    extra = jnp.concatenate([hi, mid, lo, jnp.zeros((5, LANES), F32)], axis=0)
    rows = send_ref.shape[1] - 8
    for r in range(send_ref.shape[0]):
        send_ref[r] = jnp.concatenate([wgrad[r * rows : (r + 1) * rows, :], extra], axis=0).astype(BF16)


def sum_plane_kernel(x_ref, out_ref):
    out_ref[...] = jnp.sum(x_ref[...].astype(F32), axis=0)


def write_kernel(qgrad_ref, pgrad_ref, after_ref, qgrad_hbm, pgrad_hbm, done_ref, sem):
    copies = [
        pltpu.make_async_copy(qgrad_ref, qgrad_hbm, sem.at[0]),
        pltpu.make_async_copy(pgrad_ref, pgrad_hbm, sem.at[1]),
    ]
    for copy in copies:
        copy.start()
    done_ref[...] = after_ref[:8, :]
    for copy in copies:
        copy.wait()


def sum_pair_kernel(x_ref, y_ref, done_ref, out_ref):
    y = x_ref[...] + y_ref[...]
    rows = y.shape[0] - 8
    hi, mid, lo = split3(jnp.sum(y[rows:], axis=0, keepdims=True))
    y = jnp.concatenate([y[:rows], hi, mid, lo, jnp.zeros((5, LANES), F32)], axis=0).astype(BF16)
    for c in range(out_ref.shape[0]):
        out_ref[c] = y


def sum_column_kernel(total, x_ref, out_ref, loss_ref):
    y = jnp.sum(x_ref[...].astype(F32), axis=0)
    rows = out_ref.shape[1]
    z = y[:rows].astype(BF16)
    for c in range(out_ref.shape[0]):
        out_ref[c] = z
    loss_ref[...] = jnp.broadcast_to(jnp.sum(y[rows:], axis=0, keepdims=True) / total, loss_ref.shape)


def final_kernel(x_ref, loss_in_ref, out_ref, loss_ref):
    rows = x_ref.shape[1]
    loss_ref[...] = loss_in_ref[:1, :]
    for c in range(x_ref.shape[0]):
        out_ref[c * rows : (c + 1) * rows, :] = x_ref[c].astype(F32)


VM = pl.BlockSpec(memory_space=pltpu.VMEM)
HBM = pl.BlockSpec(memory_space=pltpu.HBM)
FAR = pl.BlockSpec(memory_space=pltpu.VMEM)


def call(name, kernel, ins, out_shape, *args, outs=None, scratch=(), flops=0, bytes_accessed=0):
    args = [pltpu.with_memory_space_constraint(a, pltpu.HBM) if i is HBM or i is FAR else a for a, i in zip(args, ins)]
    return pl.pallas_call(
        kernel,
        name=name,
        out_shape=out_shape,
        in_specs=ins,
        out_specs=outs or jax.tree.map(lambda _: VM, out_shape),
        scratch_shapes=scratch,
        compiler_params=pltpu.CompilerParams(vmem_limit_bytes=32 << 20),
        cost_estimate=pl.CostEstimate(flops=flops, bytes_accessed=bytes_accessed, transcendentals=0),
    )(*args)


def query_call(qhid, projection, nblk):
    mine, hidden = qhid.shape
    dim = projection.shape[1]
    return call(
        "query_tokens", query_kernel, [FAR, FAR], pltpu.VMEM((nblk, dim, mine), BF16), qhid, projection,
        flops=2 * mine * hidden * dim, bytes_accessed=400_000,
    )


def passage_call(lengths, phid, projection, nblk):
    npass, plen, hidden = phid.shape
    dim = projection.shape[1]
    S = jax.ShapeDtypeStruct
    return call(
        "passage_tokens", passage_kernel, [HBM, HBM, HBM],
        (S((npass, 2, plen, dim), BF16), S((npass + 1, nblk, LANES), jnp.int32)),
        lengths, phid, projection,
        scratch=[pltpu.VMEM((npass, plen, hidden), BF16), pltpu.VMEM((hidden, dim), BF16),
                 pltpu.SMEM(lengths.shape, jnp.int32), pltpu.SemaphoreType.DMA((npass + 2,))],
        flops=2 * npass * plen * hidden * dim, bytes_accessed=8_000_000,
    )


def score_call(qt, tok, tab, phid, qlen):
    nblk, dim, _ = qt.shape
    npass, _, plen, _ = tok.shape
    ntok = nblk * LANES
    S = jax.ShapeDtypeStruct
    return call(
        "scores", functools.partial(score_kernel, qlen), [VM] * 3 + [HBM],
        (S((npass, plen, ntok), BF16), S((2, npass, nblk, LANES), F32), S((nblk, dim + EXTRA, LANES), BF16),
         S((npass, dim, LANES), F32), S(phid.shape, BF16)),
        qt, tok, tab, phid,
        scratch=[pltpu.VMEM((dim, ntok), BF16), pltpu.VMEM((2, plen, ntok), F32),
                 pltpu.VMEM((npass, nblk, dim, LANES), F32), pltpu.VMEM((8, ntok), F32),
                 pltpu.SemaphoreType.DMA((2,))],
        flops=4 * npass * plen * ntok * dim, bytes_accessed=8_000_000,
    )


def grad_call(tab, recv, e, stat, own, qt, phid, qhid, qlen, total, nplane):
    npass, plen, ntok = e.shape
    mine, hidden = qhid.shape
    dim = qt.shape[1]
    rows = hidden // nplane
    S = jax.ShapeDtypeStruct
    return call(
        "grads", functools.partial(grad_kernel, qlen, total), [VM] * 8,
        (pltpu.VMEM((mine, dim), F32), pltpu.VMEM((npass, plen, dim), F32), S((nplane, rows + 8, dim), BF16)),
        tab, recv, e, stat, own, qt, phid, qhid,
        scratch=[pltpu.VMEM((dim, hidden), F32), pltpu.VMEM((2, dim, ntok), BF16), pltpu.VMEM((npass * plen, dim), BF16)],
        flops=2 * npass * plen * ntok * dim, bytes_accessed=8_000_000,
    )


def shards(query_hidden, passage_hidden, lengths, projection):
    hidden, dim = projection.shape
    nquery, qlen = query_hidden.shape[1:3]
    npass, plen = passage_hidden.shape[1:3]
    nblk, nrep = lax.axis_size(BLK), lax.axis_size(REP)
    nplane, ncolumn = lax.axis_size(PLANE), lax.axis_size(COLUMN)
    total = nblk * nrep * nquery
    mine = nquery * qlen
    ntok = nblk * mine
    rows = hidden // nplane
    qflat = query_hidden[0].reshape(-1, hidden)
    S = jax.ShapeDtypeStruct

    copies = query_call(qflat, projection, nblk)
    qt = lax.all_to_all(copies, BLK, 0, 0)
    tok, tab = passage_call(lengths, passage_hidden[0], projection, nblk)
    e, stat, send, own, phid = score_call(qt, tok, tab, passage_hidden[0], qlen)
    recv = lax.all_to_all(send, BLK, 0, 0)
    qgrad, pgrad, send = grad_call(tab, recv, e, stat, own, qt, phid, qflat, qlen, float(total), nplane)
    part = lax.all_to_all(send, PLANE, 0, 0)
    part = call("sum_plane", sum_plane_kernel, [VM], S((rows + 8, dim), F32), part)
    twin = lax.ppermute(part, "core", [(0, 1), (1, 0)])
    qgrad, pgrad, done = call(
        "write_out", write_kernel, [VM, VM, VM],
        (S((mine, dim), F32), S((npass, plen, dim), F32), S((8, dim), F32)), qgrad, pgrad, part,
        outs=(HBM, HBM, VM), scratch=[pltpu.SemaphoreType.DMA((2,))], bytes_accessed=2_000_000,
    )
    part = call("sum_pair", sum_pair_kernel, [VM, VM, VM], S((ncolumn, rows + 8, dim), BF16), part, twin, done)
    part = lax.all_to_all(part, COLUMN, 0, 0)
    part, loss = call(
        "sum_column", functools.partial(sum_column_kernel, float(total)), [VM],
        (S((nplane, rows, dim), BF16), S((8, dim), F32)), part,
    )
    part = lax.all_to_all(part, PLANE, 0, 0)
    wgrad, loss = call("final", final_kernel, [VM, VM], (S((hidden, dim), F32), S((1, dim), F32)), part, loss)
    return (
        qgrad.reshape(1, nquery, qlen, dim),
        pgrad.reshape(1, npass, plen, dim),
        wgrad,
        loss[0, 0],
    )


def solution(mesh):
    fine = Mesh(mesh.devices.reshape(2, 4, 8, 2, 2), AXES)
    return jax.shard_map(
        shards,
        mesh=fine,
        in_specs=(P(REP, BLK, None, None), P(REP, BLK, None, None), P(REP, BLK), P()),
        out_specs=(P(REP, BLK, None, None), P(REP, BLK, None, None), P(), P()),
        check_vma=False,
    )
```

```python
import functools
import math

import jax
import jax.numpy as jnp
from jax import lax
from jax.experimental import pallas as pl
from jax.experimental.pallas import tpu as pltpu
from jax.sharding import Mesh
from jax.sharding import PartitionSpec as P

F32 = jnp.float32
BF16 = jnp.bfloat16
INV_TEMPER = 2.0
TEMPER = 0.5
EXP2_SCALE = INV_TEMPER * math.log2(math.e)
LANES = 128
EXTRA = 8
AXES = ("x_hi", "y", "z", "x_lo", "core")
BLK = ("x_hi", "y")
REP = ("z", "x_lo", "core")
PLANE = ("x_hi", "y", "x_lo")
COLUMN = "z"
NN = (((1,), (0,)), ((), ()))
NT = (((1,), (1,)), ((), ()))
TN = (((0,), (0,)), ((), ()))


def mm(a, b, dims):
    return lax.dot_general(a, b, dims, preferred_element_type=F32)


def to_row(x):
    return jnp.concatenate([x[c : c + 1, :] for c in range(x.shape[0])], axis=1)


def to_chunks(x):
    n = x.shape[1] // LANES
    return jnp.concatenate([x[:, c * LANES : (c + 1) * LANES] for c in range(n)], axis=0)


def split3(x):
    hi = x.astype(BF16).astype(F32)
    rest = x - hi
    mid = rest.astype(BF16).astype(F32)
    return hi, mid, (rest - mid)


def segment_sum(x, width):
    lane = lax.broadcasted_iota(jnp.int32, x.shape, 1)
    step = 1
    while step < width:
        up = pltpu.roll(x, x.shape[1] - step, 1)
        down = pltpu.roll(x, step, 1)
        x = x + jnp.where((lane & step) == 0, up, down)
        step *= 2
    return x


def query_kernel(q_ref, w_ref, out_ref):
    tok = mm(q_ref[...], w_ref[...], NN)
    flipped = tok.T.astype(BF16)
    for c in range(out_ref.shape[0]):
        out_ref[c] = flipped


def passage_kernel(len_hbm, phid_hbm, w_hbm, tok_ref, tab_ref, phid_ref, w_ref, len_ref, sem):
    npass = phid_ref.shape[0]
    lens = pltpu.make_async_copy(len_hbm, len_ref, sem.at[npass + 1])
    lens.start()
    copies = [pltpu.make_async_copy(w_hbm, w_ref, sem.at[npass])]
    half = npass // 2
    for k, at in enumerate((pl.ds(0, half), pl.ds(half, npass - half))):
        copies.append(pltpu.make_async_copy(phid_hbm.at[at], phid_ref.at[at], sem.at[k]))
    for copy in copies:
        copy.start()
    shape = tab_ref.shape[1:]
    tab_ref[npass] = jnp.full(shape, lax.axis_index("x_hi") * lax.axis_size("y") + lax.axis_index("y"), jnp.int32)
    lens.wait()
    for p in range(npass):
        tab_ref[p] = jnp.full(shape, len_ref[0, p], jnp.int32)
    copies[0].wait()
    for p in range(npass):
        if p == 0:
            copies[1].wait()
        if p == half:
            copies[2].wait()
        tok = mm(phid_ref[p], w_ref[...], NN)
        tok_ref[p, 0] = tok.astype(BF16)
        for r in range(0, tok.shape[0], LANES):
            tok_ref[p, 1, r : r + LANES, :] = tok[r : r + LANES, :].T.astype(BF16)


def score_kernel(
    qlen, qt_ref, tok_ref, tab_ref, phid_hbm, e_ref, stat_ref, send_ref, own_ref, phid_ref,
    qs_ref, s_ref, g_ref, top_ref, sem,
):
    copies = [
        pltpu.make_async_copy(phid_hbm, phid_ref, sem.at[0]),
    ]
    for copy in copies:
        copy.start()
    nblk = qt_ref.shape[0]
    npass, slots, ntok = e_ref.shape
    for c in range(nblk):
        qs_ref[:, c * LANES : (c + 1) * LANES] = qt_ref[c]
    rows = 128

    def fold(x, op):
        return functools.reduce(op, [x[r : r + 8] for r in range(0, x.shape[0], 8)])

    def scores(p):
        top = None
        count = tab_ref[p, :1, :1]
        for r in range(0, slots, rows):
            x = mm(tok_ref[p, 0, r : r + rows, :], qs_ref[...], NN)
            row = lax.broadcasted_iota(jnp.int32, (rows, 1), 0) + r
            x = jnp.where(row < count, x, -jnp.inf)
            s_ref[p % 2, r : r + rows, :] = x
            high = fold(x, jnp.maximum)
            top = high if top is None else jnp.maximum(top, high)
        return jnp.max(top, axis=0, keepdims=True)

    def powers(p, top):
        total = jnp.zeros((8, ntok), F32)
        top_ref[...] = jnp.broadcast_to(top, (8, ntok))
        wide = top_ref[...]
        for r in range(0, slots, 16):
            parts = [jnp.exp2((s_ref[p % 2, q : q + 8, :] - wide) * EXP2_SCALE) for q in (r, r + 8)]
            total = total + (parts[0] + parts[1])
            e_ref[p, r : r + 16, :] = jnp.concatenate(parts, axis=0).astype(BF16)
        return jnp.sum(total, axis=0, keepdims=True)

    def finish(p, top, total):
        inv = 1.0 / total
        logz = to_chunks(top * INV_TEMPER + jnp.log(total))
        log_count = jnp.log(tab_ref[p].astype(F32))
        stat_ref[0, p] = segment_sum(TEMPER * (logz - log_count), qlen)
        stat_ref[1, p] = to_chunks(inv)
        flipped = jnp.concatenate([tok_ref[p, 1, r : r + LANES, :] for r in range(0, slots, LANES)], axis=1)
        g = mm(flipped, e_ref[p], NN) * inv
        for c in range(nblk):
            g_ref[p, c] = g[:, c * LANES : (c + 1) * LANES]

    top = scores(0)
    for p in range(npass):
        after = scores(p + 1) if p + 1 < npass else None
        total = powers(p, top)
        finish(p, top, total)
        top = after

    score = [stat_ref[0, k] for k in range(npass)]
    high = functools.reduce(jnp.maximum, score)
    lse = high + jnp.log(sum(jnp.exp(s - high) for s in score))
    share = [jnp.exp(s - lse) for s in score]
    hi, mid, lo = split3(lse)
    place = lax.broadcasted_iota(jnp.int32, lse.shape, 1) % 4
    extra = jnp.where(place == 0, hi, jnp.where(place == 1, mid, jnp.where(place == 2, lo, 0.0))).astype(BF16)
    me = tab_ref[npass, :1, :1]
    own = [jnp.zeros(own_ref.shape[1:], F32) for _ in range(npass)]
    for c in range(nblk):
        part = jnp.zeros(own_ref.shape[1:], F32)
        for k in range(npass):
            g = g_ref[k, c]
            part = part + g * share[k][c : c + 1, :]
            own[k] = jnp.where(me == c, g, own[k])
        send_ref[c, :LANES, :] = part.astype(BF16)
        send_ref[c, LANES:, :] = extra
    for k in range(npass):
        own_ref[k] = own[k]
    for copy in copies:
        copy.wait()


def grad_kernel(
    qlen, total, tab_ref, recv_ref, e_ref, stat_ref, own_ref, qt_ref, phid_ref, qhid_ref,
    qgrad_ref, pgrad_ref, send_ref, acc_ref, qs_ref, small_ref,
):
    nblk = qt_ref.shape[0]
    npass = stat_ref.shape[1]
    me = tab_ref[npass, :1, :1]
    lane = lax.broadcasted_iota(jnp.int32, (nblk, LANES), 1)
    chunk = lax.broadcasted_iota(jnp.int32, (nblk, LANES), 0)
    mine = chunk == me

    def pick(x):
        return jnp.sum(jnp.where(mine, x, 0.0), axis=0, keepdims=True)

    parts = []
    for d in range(nblk):
        parts.append(segment_sum(recv_ref[d, LANES:, :].astype(F32), 4))
    high = functools.reduce(jnp.maximum, parts)
    lse = high + jnp.log(sum(jnp.exp(x - high) for x in parts))
    dscore = []
    loss = jnp.zeros((nblk, LANES), F32)
    for k in range(npass):
        hit = mine & (lane // qlen == k)
        dscore.append((jnp.exp(stat_ref[0, k] - lse) - hit.astype(F32)) / total)
        loss = loss + jnp.where(mine & (lane == k * qlen), lse - stat_ref[0, k], 0.0)

    for p in range(npass):
        weight = dscore[p] * stat_ref[1, p]
        for c in range(nblk):
            qs_ref[p % 2, :, c * LANES : (c + 1) * LANES] = (
                qt_ref[c].astype(F32) * weight[c : c + 1, :]
            ).astype(BF16)
        pgrad = mm(e_ref[p], qs_ref[p % 2], NT)
        pgrad_ref[p] = pgrad
        small_ref[p * pgrad.shape[0] : (p + 1) * pgrad.shape[0], :] = pgrad.astype(BF16)
    acc_ref[...] = mm(small_ref[...], phid_ref[...].reshape(small_ref.shape[0], -1), TN)
    grad = jnp.zeros((LANES, LANES), F32)
    for k in range(npass):
        grad = grad + own_ref[k] * pick(dscore[k])
    for d in range(nblk):
        share = jnp.where(me == d, 0.0, pick(jnp.exp(parts[d] - lse)) / total)
        grad = grad + recv_ref[d, :LANES, :].astype(F32) * share
    qgrad_ref[...] = grad.T
    wgrad = (acc_ref[...] + mm(grad.astype(BF16), qhid_ref[...], NN)).T


    hi, mid, lo = split3(jnp.full((1, LANES), jnp.sum(loss)))
    extra = jnp.concatenate([hi, mid, lo, jnp.zeros((5, LANES), F32)], axis=0)
    rows = send_ref.shape[1] - 8
    for r in range(send_ref.shape[0]):
        send_ref[r] = jnp.concatenate([wgrad[r * rows : (r + 1) * rows, :], extra], axis=0).astype(BF16)


def sum_plane_kernel(x_ref, out_ref):
    out_ref[...] = jnp.sum(x_ref[...].astype(F32), axis=0)


def write_kernel(qgrad_ref, pgrad_ref, after_ref, qgrad_hbm, pgrad_hbm, done_ref, sem):
    copies = [
        pltpu.make_async_copy(qgrad_ref, qgrad_hbm, sem.at[0]),
        pltpu.make_async_copy(pgrad_ref, pgrad_hbm, sem.at[1]),
    ]
    for copy in copies:
        copy.start()
    done_ref[...] = after_ref[:8, :]
    for copy in copies:
        copy.wait()


def sum_pair_kernel(x_ref, y_ref, done_ref, out_ref):
    y = x_ref[...] + y_ref[...]
    rows = y.shape[0] - 8
    hi, mid, lo = split3(jnp.sum(y[rows:], axis=0, keepdims=True))
    y = jnp.concatenate([y[:rows], hi, mid, lo, jnp.zeros((5, LANES), F32)], axis=0).astype(BF16)
    for c in range(out_ref.shape[0]):
        out_ref[c] = y


def sum_column_kernel(total, x_ref, out_ref, loss_ref):
    y = jnp.sum(x_ref[...].astype(F32), axis=0)
    rows = out_ref.shape[1]
    z = y[:rows].astype(BF16)
    for c in range(out_ref.shape[0]):
        out_ref[c] = z
    loss_ref[...] = jnp.broadcast_to(jnp.sum(y[rows:], axis=0, keepdims=True) / total, loss_ref.shape)


def final_kernel(x_ref, loss_in_ref, out_ref, loss_ref):
    rows = x_ref.shape[1]
    loss_ref[...] = loss_in_ref[:1, :]
    for c in range(x_ref.shape[0]):
        out_ref[c * rows : (c + 1) * rows, :] = x_ref[c].astype(F32)


VM = pl.BlockSpec(memory_space=pltpu.VMEM)
HBM = pl.BlockSpec(memory_space=pltpu.HBM)
FAR = pl.BlockSpec(memory_space=pltpu.VMEM)


def call(name, kernel, ins, out_shape, *args, outs=None, scratch=(), flops=0, bytes_accessed=0):
    args = [pltpu.with_memory_space_constraint(a, pltpu.HBM) if i is HBM or i is FAR else a for a, i in zip(args, ins)]
    return pl.pallas_call(
        kernel,
        name=name,
        out_shape=out_shape,
        in_specs=ins,
        out_specs=outs or jax.tree.map(lambda _: VM, out_shape),
        scratch_shapes=scratch,
        compiler_params=pltpu.CompilerParams(vmem_limit_bytes=32 << 20),
        cost_estimate=pl.CostEstimate(flops=flops, bytes_accessed=bytes_accessed, transcendentals=0),
    )(*args)


def query_call(qhid, projection, nblk):
    mine, hidden = qhid.shape
    dim = projection.shape[1]
    return call(
        "query_tokens", query_kernel, [FAR, FAR], pltpu.VMEM((nblk, dim, mine), BF16), qhid, projection,
        flops=2 * mine * hidden * dim, bytes_accessed=400_000,
    )


def passage_call(lengths, phid, projection, nblk):
    npass, plen, hidden = phid.shape
    dim = projection.shape[1]
    S = jax.ShapeDtypeStruct
    return call(
        "passage_tokens", passage_kernel, [HBM, HBM, HBM],
        (S((npass, 2, plen, dim), BF16), S((npass + 1, nblk, LANES), jnp.int32)),
        lengths, phid, projection,
        scratch=[pltpu.VMEM((npass, plen, hidden), BF16), pltpu.VMEM((hidden, dim), BF16),
                 pltpu.SMEM(lengths.shape, jnp.int32), pltpu.SemaphoreType.DMA((npass + 2,))],
        flops=2 * npass * plen * hidden * dim, bytes_accessed=8_000_000,
    )


def score_call(qt, tok, tab, phid, qlen):
    nblk, dim, _ = qt.shape
    npass, _, plen, _ = tok.shape
    ntok = nblk * LANES
    S = jax.ShapeDtypeStruct
    return call(
        "scores", functools.partial(score_kernel, qlen), [VM] * 3 + [HBM],
        (S((npass, plen, ntok), BF16), S((2, npass, nblk, LANES), F32), S((nblk, dim + EXTRA, LANES), BF16),
         S((npass, dim, LANES), F32), S(phid.shape, BF16)),
        qt, tok, tab, phid,
        scratch=[pltpu.VMEM((dim, ntok), BF16), pltpu.VMEM((2, plen, ntok), F32),
                 pltpu.VMEM((npass, nblk, dim, LANES), F32), pltpu.VMEM((8, ntok), F32),
                 pltpu.SemaphoreType.DMA((2,))],
        flops=4 * npass * plen * ntok * dim, bytes_accessed=8_000_000,
    )


def grad_call(tab, recv, e, stat, own, qt, phid, qhid, qlen, total, nplane):
    npass, plen, ntok = e.shape
    mine, hidden = qhid.shape
    dim = qt.shape[1]
    rows = hidden // nplane
    S = jax.ShapeDtypeStruct
    return call(
        "grads", functools.partial(grad_kernel, qlen, total), [VM] * 8,
        (pltpu.VMEM((mine, dim), F32), pltpu.VMEM((npass, plen, dim), F32), S((nplane, rows + 8, dim), BF16)),
        tab, recv, e, stat, own, qt, phid, qhid,
        scratch=[pltpu.VMEM((dim, hidden), F32), pltpu.VMEM((2, dim, ntok), BF16), pltpu.VMEM((npass * plen, dim), BF16)],
        flops=2 * npass * plen * ntok * dim, bytes_accessed=8_000_000,
    )


def shards(query_hidden, passage_hidden, lengths, projection):
    hidden, dim = projection.shape
    nquery, qlen = query_hidden.shape[1:3]
    npass, plen = passage_hidden.shape[1:3]
    nblk, nrep = lax.axis_size(BLK), lax.axis_size(REP)
    nplane, ncolumn = lax.axis_size(PLANE), lax.axis_size(COLUMN)
    total = nblk * nrep * nquery
    mine = nquery * qlen
    ntok = nblk * mine
    rows = hidden // nplane
    qflat = query_hidden[0].reshape(-1, hidden)
    S = jax.ShapeDtypeStruct

    copies = query_call(qflat, projection, nblk)
    qt = lax.all_to_all(copies, BLK, 0, 0)
    tok, tab = passage_call(lengths, passage_hidden[0], projection, nblk)
    e, stat, send, own, phid = score_call(qt, tok, tab, passage_hidden[0], qlen)
    recv = lax.all_to_all(send, BLK, 0, 0)
    qgrad, pgrad, send = grad_call(tab, recv, e, stat, own, qt, phid, qflat, qlen, float(total), nplane)
    part = lax.all_to_all(send, PLANE, 0, 0)
    part = call("sum_plane", sum_plane_kernel, [VM], S((rows + 8, dim), F32), part)
    twin = lax.ppermute(part, "core", [(0, 1), (1, 0)])
    qgrad, pgrad, done = call(
        "write_out", write_kernel, [VM, VM, VM],
        (S((mine, dim), F32), S((npass, plen, dim), F32), S((8, dim), F32)), qgrad, pgrad, part,
        outs=(HBM, HBM, VM), scratch=[pltpu.SemaphoreType.DMA((2,))], bytes_accessed=2_000_000,
    )
    part = call("sum_pair", sum_pair_kernel, [VM, VM, VM], S((ncolumn, rows + 8, dim), BF16), part, twin, done)
    part = lax.all_to_all(part, COLUMN, 0, 0)
    part, loss = call(
        "sum_column", functools.partial(sum_column_kernel, float(total)), [VM],
        (S((nplane, rows, dim), BF16), S((8, dim), F32)), part,
    )
    part = lax.all_to_all(part, PLANE, 0, 0)
    wgrad, loss = call("final", final_kernel, [VM, VM], (S((hidden, dim), F32), S((1, dim), F32)), part, loss)
    return (
        qgrad.reshape(1, nquery, qlen, dim),
        pgrad.reshape(1, npass, plen, dim),
        wgrad,
        loss[0, 0],
    )


def solution(mesh):
    fine = Mesh(mesh.devices.reshape(2, 4, 8, 2, 2), AXES)
    return jax.shard_map(
        shards,
        mesh=fine,
        in_specs=(P(REP, BLK, None, None), P(REP, BLK, None, None), P(REP, BLK), P()),
        out_specs=(P(REP, BLK, None, None), P(REP, BLK, None, None), P(), P()),
        check_vma=False,
    )
```

```python
import functools
import math

import jax
import jax.numpy as jnp
from jax import lax
from jax.experimental import pallas as pl
from jax.experimental.pallas import tpu as pltpu
from jax.sharding import Mesh
from jax.sharding import PartitionSpec as P

F32 = jnp.float32
BF16 = jnp.bfloat16
INV_TEMPER = 2.0
TEMPER = 0.5
EXP2_SCALE = INV_TEMPER * math.log2(math.e)
LANES = 128
EXTRA = 8
AXES = ("x_hi", "y", "z", "x_lo", "core")
BLK = ("x_hi", "y")
REP = ("z", "x_lo", "core")
PLANE = ("x_hi", "y", "x_lo")
COLUMN = "z"
NN = (((1,), (0,)), ((), ()))
NT = (((1,), (1,)), ((), ()))
TN = (((0,), (0,)), ((), ()))


def mm(a, b, dims):
    return lax.dot_general(a, b, dims, preferred_element_type=F32)


def to_row(x):
    return jnp.concatenate([x[c : c + 1, :] for c in range(x.shape[0])], axis=1)


def to_chunks(x):
    n = x.shape[1] // LANES
    return jnp.concatenate([x[:, c * LANES : (c + 1) * LANES] for c in range(n)], axis=0)


def split3(x):
    hi = x.astype(BF16).astype(F32)
    rest = x - hi
    mid = rest.astype(BF16).astype(F32)
    return hi, mid, (rest - mid)


def segment_sum(x, width):
    lane = lax.broadcasted_iota(jnp.int32, x.shape, 1)
    step = 1
    while step < width:
        up = pltpu.roll(x, x.shape[1] - step, 1)
        down = pltpu.roll(x, step, 1)
        x = x + jnp.where((lane & step) == 0, up, down)
        step *= 2
    return x


def query_kernel(q_ref, w_ref, out_ref):
    tok = mm(q_ref[...], w_ref[...], NN)
    flipped = tok.T.astype(BF16)
    for c in range(out_ref.shape[0]):
        out_ref[c] = flipped


def passage_kernel(len_hbm, phid_hbm, w_hbm, tok_ref, tab_ref, phid_ref, w_ref, len_ref, sem):
    npass = phid_ref.shape[0]
    lens = pltpu.make_async_copy(len_hbm, len_ref, sem.at[npass + 1])
    lens.start()
    copies = [pltpu.make_async_copy(w_hbm, w_ref, sem.at[npass])]
    half = npass // 2
    for k, at in enumerate((pl.ds(0, half), pl.ds(half, npass - half))):
        copies.append(pltpu.make_async_copy(phid_hbm.at[at], phid_ref.at[at], sem.at[k]))
    for copy in copies:
        copy.start()
    shape = tab_ref.shape[1:]
    tab_ref[npass] = jnp.full(shape, lax.axis_index("x_hi") * lax.axis_size("y") + lax.axis_index("y"), jnp.int32)
    lens.wait()
    for p in range(npass):
        tab_ref[p] = jnp.full(shape, len_ref[0, p], jnp.int32)
    copies[0].wait()
    for p in range(npass):
        if p == 0:
            copies[1].wait()
        if p == half:
            copies[2].wait()
        tok = mm(phid_ref[p], w_ref[...], NN)
        tok_ref[p, 0] = tok.astype(BF16)
        for r in range(0, tok.shape[0], LANES):
            tok_ref[p, 1, r : r + LANES, :] = tok[r : r + LANES, :].T.astype(BF16)


def score_kernel(
    qlen, qt_ref, tok_ref, tab_ref, phid_hbm, e_ref, stat_ref, send_ref, own_ref, phid_ref,
    qs_ref, s_ref, g_ref, top_ref, sem,
):
    copies = [
        pltpu.make_async_copy(phid_hbm, phid_ref, sem.at[0]),
    ]
    for copy in copies:
        copy.start()
    nblk = qt_ref.shape[0]
    npass, slots, ntok = e_ref.shape
    for c in range(nblk):
        qs_ref[:, c * LANES : (c + 1) * LANES] = qt_ref[c]
    rows = 128

    def fold(x, op):
        return functools.reduce(op, [x[r : r + 8] for r in range(0, x.shape[0], 8)])

    def scores(p):
        top = None
        count = tab_ref[p, :1, :1]
        for r in range(0, slots, rows):
            x = mm(tok_ref[p, 0, r : r + rows, :], qs_ref[...], NN)
            row = lax.broadcasted_iota(jnp.int32, (rows, 1), 0) + r
            x = jnp.where(row < count, x, -jnp.inf)
            s_ref[p % 2, r : r + rows, :] = x
            high = fold(x, jnp.maximum)
            top = high if top is None else jnp.maximum(top, high)
        return jnp.max(top, axis=0, keepdims=True)

    def powers(p, top):
        total = jnp.zeros((8, ntok), F32)
        top_ref[...] = jnp.broadcast_to(top, (8, ntok))
        wide = top_ref[...]
        for r in range(0, slots, 16):
            parts = [jnp.exp2((s_ref[p % 2, q : q + 8, :] - wide) * EXP2_SCALE) for q in (r, r + 8)]
            total = total + (parts[0] + parts[1])
            e_ref[p, r : r + 16, :] = jnp.concatenate(parts, axis=0).astype(BF16)
        return jnp.sum(total, axis=0, keepdims=True)

    def finish(p, top, total):
        inv = 1.0 / total
        logz = to_chunks(top * INV_TEMPER + jnp.log(total))
        log_count = jnp.log(tab_ref[p].astype(F32))
        stat_ref[0, p] = segment_sum(TEMPER * (logz - log_count), qlen)
        stat_ref[1, p] = to_chunks(inv)
        flipped = jnp.concatenate([tok_ref[p, 1, r : r + LANES, :] for r in range(0, slots, LANES)], axis=1)
        g = mm(flipped, e_ref[p], NN) * inv
        for c in range(nblk):
            g_ref[p, c] = g[:, c * LANES : (c + 1) * LANES]

    top = scores(0)
    for p in range(npass):
        after = scores(p + 1) if p + 1 < npass else None
        total = powers(p, top)
        finish(p, top, total)
        top = after

    score = [stat_ref[0, k] for k in range(npass)]
    high = functools.reduce(jnp.maximum, score)
    lse = high + jnp.log(sum(jnp.exp(s - high) for s in score))
    share = [jnp.exp(s - lse) for s in score]
    hi, mid, lo = split3(lse)
    place = lax.broadcasted_iota(jnp.int32, lse.shape, 1) % 4
    extra = jnp.where(place == 0, hi, jnp.where(place == 1, mid, jnp.where(place == 2, lo, 0.0))).astype(BF16)
    me = tab_ref[npass, :1, :1]
    own = [jnp.zeros(own_ref.shape[1:], F32) for _ in range(npass)]
    for c in range(nblk):
        part = jnp.zeros(own_ref.shape[1:], F32)
        for k in range(npass):
            g = g_ref[k, c]
            part = part + g * share[k][c : c + 1, :]
            own[k] = jnp.where(me == c, g, own[k])
        send_ref[c, :LANES, :] = part.astype(BF16)
        send_ref[c, LANES:, :] = extra
    for k in range(npass):
        own_ref[k] = own[k]
    for copy in copies:
        copy.wait()


def grad_kernel(
    qlen, total, tab_ref, recv_ref, e_ref, stat_ref, own_ref, qt_ref, phid_ref, qhid_ref,
    qgrad_ref, pgrad_ref, send_ref, qs_ref, small_ref,
):
    nblk = qt_ref.shape[0]
    npass = stat_ref.shape[1]
    me = tab_ref[npass, :1, :1]
    lane = lax.broadcasted_iota(jnp.int32, (nblk, LANES), 1)
    chunk = lax.broadcasted_iota(jnp.int32, (nblk, LANES), 0)
    mine = chunk == me

    def pick(x):
        return jnp.sum(jnp.where(mine, x, 0.0), axis=0, keepdims=True)

    parts = []
    for d in range(nblk):
        parts.append(segment_sum(recv_ref[d, LANES:, :].astype(F32), 4))
    high = functools.reduce(jnp.maximum, parts)
    lse = high + jnp.log(sum(jnp.exp(x - high) for x in parts))
    dscore = []
    loss = jnp.zeros((nblk, LANES), F32)
    for k in range(npass):
        hit = mine & (lane // qlen == k)
        dscore.append((jnp.exp(stat_ref[0, k] - lse) - hit.astype(F32)) / total)
        loss = loss + jnp.where(mine & (lane == k * qlen), lse - stat_ref[0, k], 0.0)

    for p in range(npass):
        weight = dscore[p] * stat_ref[1, p]
        for c in range(nblk):
            qs_ref[p % 2, :, c * LANES : (c + 1) * LANES] = (
                qt_ref[c].astype(F32) * weight[c : c + 1, :]
            ).astype(BF16)
        pgrad = mm(e_ref[p], qs_ref[p % 2], NT)
        pgrad_ref[p] = pgrad
        small_ref[p * pgrad.shape[0] : (p + 1) * pgrad.shape[0], :] = pgrad.astype(BF16)
    terms = mm(small_ref[...], phid_ref[...].reshape(small_ref.shape[0], -1), TN)
    grad = jnp.zeros((LANES, LANES), F32)
    for k in range(npass):
        grad = grad + own_ref[k] * pick(dscore[k])
    for d in range(nblk):
        share = jnp.where(me == d, 0.0, pick(jnp.exp(parts[d] - lse)) / total)
        grad = grad + recv_ref[d, :LANES, :].astype(F32) * share
    qgrad_ref[...] = grad.T
    wgrad = (terms + mm(grad.astype(BF16), qhid_ref[...], NN)).T


    hi, mid, lo = split3(jnp.full((1, LANES), jnp.sum(loss)))
    extra = jnp.concatenate([hi, mid, lo, jnp.zeros((5, LANES), F32)], axis=0)
    rows = send_ref.shape[1] - 8
    for r in range(send_ref.shape[0]):
        send_ref[r] = jnp.concatenate([wgrad[r * rows : (r + 1) * rows, :], extra], axis=0).astype(BF16)


def sum_plane_kernel(x_ref, out_ref):
    out_ref[...] = jnp.sum(x_ref[...].astype(F32), axis=0)


def write_kernel(qgrad_ref, pgrad_ref, after_ref, qgrad_hbm, pgrad_hbm, done_ref, sem):
    copies = [
        pltpu.make_async_copy(qgrad_ref, qgrad_hbm, sem.at[0]),
        pltpu.make_async_copy(pgrad_ref, pgrad_hbm, sem.at[1]),
    ]
    for copy in copies:
        copy.start()
    done_ref[...] = after_ref[:8, :]
    for copy in copies:
        copy.wait()


def sum_pair_kernel(x_ref, y_ref, done_ref, out_ref):
    y = x_ref[...] + y_ref[...]
    rows = y.shape[0] - 8
    hi, mid, lo = split3(jnp.sum(y[rows:], axis=0, keepdims=True))
    y = jnp.concatenate([y[:rows], hi, mid, lo, jnp.zeros((5, LANES), F32)], axis=0).astype(BF16)
    for c in range(out_ref.shape[0]):
        out_ref[c] = y


def sum_column_kernel(total, x_ref, out_ref, loss_ref):
    y = jnp.sum(x_ref[...].astype(F32), axis=0)
    rows = out_ref.shape[1]
    z = y[:rows].astype(BF16)
    for c in range(out_ref.shape[0]):
        out_ref[c] = z
    loss_ref[...] = jnp.broadcast_to(jnp.sum(y[rows:], axis=0, keepdims=True) / total, loss_ref.shape)


def final_kernel(x_ref, loss_in_ref, out_ref, loss_ref):
    rows = x_ref.shape[1]
    loss_ref[...] = loss_in_ref[:1, :]
    for c in range(x_ref.shape[0]):
        out_ref[c * rows : (c + 1) * rows, :] = x_ref[c].astype(F32)


VM = pl.BlockSpec(memory_space=pltpu.VMEM)
HBM = pl.BlockSpec(memory_space=pltpu.HBM)
FAR = pl.BlockSpec(memory_space=pltpu.VMEM)


def call(name, kernel, ins, out_shape, *args, outs=None, scratch=(), flops=0, bytes_accessed=0):
    args = [pltpu.with_memory_space_constraint(a, pltpu.HBM) if i is HBM or i is FAR else a for a, i in zip(args, ins)]
    return pl.pallas_call(
        kernel,
        name=name,
        out_shape=out_shape,
        in_specs=ins,
        out_specs=outs or jax.tree.map(lambda _: VM, out_shape),
        scratch_shapes=scratch,
        compiler_params=pltpu.CompilerParams(vmem_limit_bytes=32 << 20),
        cost_estimate=pl.CostEstimate(flops=flops, bytes_accessed=bytes_accessed, transcendentals=0),
    )(*args)


def query_call(qhid, projection, nblk):
    mine, hidden = qhid.shape
    dim = projection.shape[1]
    return call(
        "query_tokens", query_kernel, [FAR, FAR], pltpu.VMEM((nblk, dim, mine), BF16), qhid, projection,
        flops=2 * mine * hidden * dim, bytes_accessed=400_000,
    )


def passage_call(lengths, phid, projection, nblk):
    npass, plen, hidden = phid.shape
    dim = projection.shape[1]
    S = jax.ShapeDtypeStruct
    return call(
        "passage_tokens", passage_kernel, [HBM, HBM, HBM],
        (S((npass, 2, plen, dim), BF16), S((npass + 1, nblk, LANES), jnp.int32)),
        lengths, phid, projection,
        scratch=[pltpu.VMEM((npass, plen, hidden), BF16), pltpu.VMEM((hidden, dim), BF16),
                 pltpu.SMEM(lengths.shape, jnp.int32), pltpu.SemaphoreType.DMA((npass + 2,))],
        flops=2 * npass * plen * hidden * dim, bytes_accessed=8_000_000,
    )


def score_call(qt, tok, tab, phid, qlen):
    nblk, dim, _ = qt.shape
    npass, _, plen, _ = tok.shape
    ntok = nblk * LANES
    S = jax.ShapeDtypeStruct
    return call(
        "scores", functools.partial(score_kernel, qlen), [VM] * 3 + [HBM],
        (S((npass, plen, ntok), BF16), S((2, npass, nblk, LANES), F32), S((nblk, dim + EXTRA, LANES), BF16),
         S((npass, dim, LANES), F32), S(phid.shape, BF16)),
        qt, tok, tab, phid,
        scratch=[pltpu.VMEM((dim, ntok), BF16), pltpu.VMEM((2, plen, ntok), F32),
                 pltpu.VMEM((npass, nblk, dim, LANES), F32), pltpu.VMEM((8, ntok), F32),
                 pltpu.SemaphoreType.DMA((2,))],
        flops=4 * npass * plen * ntok * dim, bytes_accessed=8_000_000,
    )


def grad_call(tab, recv, e, stat, own, qt, phid, qhid, qlen, total, nplane):
    npass, plen, ntok = e.shape
    mine, hidden = qhid.shape
    dim = qt.shape[1]
    rows = hidden // nplane
    S = jax.ShapeDtypeStruct
    return call(
        "grads", functools.partial(grad_kernel, qlen, total), [VM] * 8,
        (pltpu.VMEM((mine, dim), F32), pltpu.VMEM((npass, plen, dim), F32), S((nplane, rows + 8, dim), BF16)),
        tab, recv, e, stat, own, qt, phid, qhid,
        scratch=[pltpu.VMEM((2, dim, ntok), BF16), pltpu.VMEM((npass * plen, dim), BF16)],
        flops=2 * npass * plen * ntok * dim, bytes_accessed=8_000_000,
    )


def shards(query_hidden, passage_hidden, lengths, projection):
    hidden, dim = projection.shape
    nquery, qlen = query_hidden.shape[1:3]
    npass, plen = passage_hidden.shape[1:3]
    nblk, nrep = lax.axis_size(BLK), lax.axis_size(REP)
    nplane, ncolumn = lax.axis_size(PLANE), lax.axis_size(COLUMN)
    total = nblk * nrep * nquery
    mine = nquery * qlen
    ntok = nblk * mine
    rows = hidden // nplane
    qflat = query_hidden[0].reshape(-1, hidden)
    S = jax.ShapeDtypeStruct

    copies = query_call(qflat, projection, nblk)
    qt = lax.all_to_all(copies, BLK, 0, 0)
    tok, tab = passage_call(lengths, passage_hidden[0], projection, nblk)
    e, stat, send, own, phid = score_call(qt, tok, tab, passage_hidden[0], qlen)
    recv = lax.all_to_all(send, BLK, 0, 0)
    qgrad, pgrad, send = grad_call(tab, recv, e, stat, own, qt, phid, qflat, qlen, float(total), nplane)
    part = lax.all_to_all(send, PLANE, 0, 0)
    part = call("sum_plane", sum_plane_kernel, [VM], S((rows + 8, dim), F32), part)
    twin = lax.ppermute(part, "core", [(0, 1), (1, 0)])
    qgrad, pgrad, done = call(
        "write_out", write_kernel, [VM, VM, VM],
        (S((mine, dim), F32), S((npass, plen, dim), F32), S((8, dim), F32)), qgrad, pgrad, part,
        outs=(HBM, HBM, VM), scratch=[pltpu.SemaphoreType.DMA((2,))], bytes_accessed=2_000_000,
    )
    part = call("sum_pair", sum_pair_kernel, [VM, VM, VM], S((ncolumn, rows + 8, dim), BF16), part, twin, done)
    part = lax.all_to_all(part, COLUMN, 0, 0)
    part, loss = call(
        "sum_column", functools.partial(sum_column_kernel, float(total)), [VM],
        (S((nplane, rows, dim), BF16), S((8, dim), F32)), part,
    )
    part = lax.all_to_all(part, PLANE, 0, 0)
    wgrad, loss = call("final", final_kernel, [VM, VM], (S((hidden, dim), F32), S((1, dim), F32)), part, loss)
    return (
        qgrad.reshape(1, nquery, qlen, dim),
        pgrad.reshape(1, npass, plen, dim),
        wgrad,
        loss[0, 0],
    )


def solution(mesh):
    fine = Mesh(mesh.devices.reshape(2, 4, 8, 2, 2), AXES)
    return jax.shard_map(
        shards,
        mesh=fine,
        in_specs=(P(REP, BLK, None, None), P(REP, BLK, None, None), P(REP, BLK), P()),
        out_specs=(P(REP, BLK, None, None), P(REP, BLK, None, None), P(), P()),
        check_vma=False,
    )
```
